256 devices in a mesh: left: 16 (over z, y_hi), right: 16 (over y_lo, x, core).
Axes of the slice: x: 4, y: 4 (y_hi: 2, y_lo: 2; y = y_hi * 2 + y_lo), z: 8, core: 2. Of those that a mesh axis runs over, the one named last changes fastest.
Arguments:
- left_table: float32 [32768, 400], P(('left', 'right')), may hold values from -2 to 2
- left_state: float32 [32768], P(('left', 'right')), may hold values from 0.05 to 0.5
- right_table: float32 [32768, 400], P(('left', 'right')), may hold values from -2 to 2
- right_state: float32 [32768], P(('left', 'right')), may hold values from 0.05 to 0.5
- relation_table: float32 [256, 400], replicated, may hold values from -6 to 6
- relation_state: float32 [256], replicated, may hold values from 0.05 to 0.5
- source_ids: int32 [16, 16, 1024], P('left', 'right'), may hold values from 0 to 2047
- target_ids: int32 [16, 16, 1024], P('left', 'right'), may hold values from 0 to 2047
- relation_ids: int32 [16, 16, 1024], P('left', 'right'), may hold values from 0 to 255
- negative_ids: int32 [16, 16, 2, 1024], P('left', 'right'), may hold values from 0 to 2047
Outputs:
- left_new: float32 [32768, 400], P(('left', 'right'))
- left_state_new: float32 [32768], P(('left', 'right'))
- right_new: float32 [32768, 400], P(('left', 'right'))
- right_state_new: float32 [32768], P(('left', 'right'))
- relation_new: float32 [256, 400], replicated
- relation_state_new: float32 [256], replicated
The draws below stay inside these ranges and needn't reach their ends.
All inputs are finite; a program needn't handle non-finite values.
Results may differ from the reference program's by a relative error of at most 0.0021.
Values may be sent and summed in bfloat16 or wider, within the bound.
A program may use at most 64 MiB of HBM per device.

```python
import math
import jax
import jax.numpy as jnp
import numpy as np
from jax import lax

EMBED_WIDTH = 400
NREL = 256
ROWS = 128
EDGES = 1024
NEG = 1024
GROUPS = 2
LEFT_ROWS = 2048
RIGHT_ROWS = 2048
ENTITIES = 32768
N_LEFT = 16
N_RIGHT = 16


def with_ends(values, own_key, low, top_value):
    extent = values.shape
    spot = [jax.random.randint(jax.random.fold_in(own_key, axis), (), 0, extent[axis]) for axis in range(len(extent))]
    values = values.at[tuple(spot)].set(low)
    longest = extent.index(max(extent))
    spot[longest] = (spot[longest] + 1) % extent[longest]
    return values.at[tuple(spot)].set(top_value)


def shard_levels(own_key, dims, split, least, high):
    factor_of = 1.0
    for dim, parts in split:
        steps = jax.random.uniform(jax.random.fold_in(jax.random.fold_in(own_key, 6), dim), (parts,), jnp.float32, least / len(split), high / len(split))
        factor_of = factor_of * jnp.repeat(jnp.exp(steps), dims[dim] // parts).reshape((-1,) + (1,) * (len(dims) - 1 - dim))
    return factor_of


def rank_table(amount, slope):
    loads = [(1 << 20) // math.isqrt(grade ** slope) + 1 for grade in range(1, amount + 1)]
    spread = 1 + sum(loads) // (1 << 30)
    return np.cumsum(np.array([max(1, weight // spread) for weight in loads]))


def skewed_ids(own_key, shape, amount, lean):
    table = rank_table(amount, lean)
    ticket = jax.random.randint(jax.random.fold_in(own_key, 1), shape, 0, int(table[amount - 1]))
    rank = jnp.searchsorted(jnp.asarray(table, jnp.int32), ticket, side="right")
    return jax.random.permutation(jax.random.fold_in(own_key, 2), amount)[rank].astype(jnp.int32)


def bell_draw(rng, extent, scale, bound, shards=(), kind=jnp.bfloat16):
    entries = jax.random.normal(rng, extent, jnp.float32) * scale
    if len(shards) > 0:
        entries = shard_levels(rng, extent, shards, -0.22, 0.18) * entries
    return jnp.clip(entries, min=-bound, max=bound).astype(kind)


def setup_inputs(seed: int = 0) -> dict:
    key_list = jax.random.split(jax.random.key(seed), 11)
    return {
        "left_table": bell_draw(key_list[0], (ENTITIES, EMBED_WIDTH), 0.3, 2.0, ((0, 256),), jnp.float32),
        "left_state": jnp.clip(jnp.exp(math.log(0.5) - 2.3025851 * jax.random.uniform(key_list[1], (ENTITIES,), jnp.float32) ** shard_levels(key_list[1], (ENTITIES,), ((0, 256),), -0.2, 0.2)), 0.05, 0.5),
        "right_table": bell_draw(key_list[2], (ENTITIES, EMBED_WIDTH), 0.3, 2.0, ((0, 256),), jnp.float32),
        "right_state": jnp.clip(jnp.exp(math.log(0.5) - 2.3025851 * jax.random.uniform(key_list[3], (ENTITIES,), jnp.float32) ** shard_levels(key_list[3], (ENTITIES,), ((0, 256),), -0.2, 0.2)), 0.05, 0.5),
        "relation_table": bell_draw(key_list[4], (NREL, EMBED_WIDTH), 1.0, 6.0, (), jnp.float32),
        "relation_state": jnp.clip(jnp.exp(jax.random.uniform(key_list[5], (NREL,), jnp.float32, math.log(0.05), math.log(0.5))), 0.05, 0.5),
        "source_ids": with_ends(jax.random.randint(key_list[6], (N_LEFT, N_RIGHT, EDGES), 0, LEFT_ROWS), jax.random.fold_in(key_list[6], 1), 0, LEFT_ROWS - 1).astype(jnp.int32),
        "target_ids": with_ends(jax.random.randint(key_list[7], (N_LEFT, N_RIGHT, EDGES), 0, RIGHT_ROWS), jax.random.fold_in(key_list[7], 1), 0, RIGHT_ROWS - 1).astype(jnp.int32),
        "relation_ids": with_ends(skewed_ids(key_list[8], (N_LEFT, N_RIGHT, EDGES), NREL, 2), jax.random.fold_in(key_list[8], 3), 0, NREL - 1).astype(jnp.int32),
        "negative_ids": with_ends(jax.random.randint(key_list[9], (N_LEFT, N_RIGHT, GROUPS, NEG), 0, RIGHT_ROWS), jax.random.fold_in(key_list[9], 1), 0, RIGHT_ROWS - 1).astype(jnp.int32),
    }


LEARN_RATE = 0.1
NEG_WEIGHT = 0.03125

def complex_product(first, second):
    half_width = first.shape[-1] // 2
    a_re, a_im = (first[..., :half_width], first[..., half_width:])
    b_re, b_im = (second[..., :half_width], second[..., half_width:])
    return jnp.concatenate([a_re * b_re - a_im * b_im, a_re * b_im + a_im * b_re], axis=-1)

def complex_back(grad, other):
    half_width = grad.shape[-1] // 2
    g_re, g_im = (grad[..., :half_width], grad[..., half_width:])
    o_re, o_im = (other[..., :half_width], other[..., half_width:])
    return jnp.concatenate([g_re * o_re + g_im * o_im, g_im * o_re - g_re * o_im], axis=-1)

def bucket_grads(left_part, right_part, relation_bf, source, target, relation, negative):
    source_emb = left_part[source].astype(jnp.float32)
    target_embedding = right_part[target].astype(jnp.float32)
    relation_emb = relation_bf[relation].astype(jnp.float32)
    query = complex_product(source_emb, relation_emb)
    positive = lax.optimization_barrier(jnp.sum(query * target_embedding, axis=-1))
    query_bf = query.astype(jnp.bfloat16)
    groups = negative.shape[0]
    query_block_rows = query_bf.reshape(groups, -1, EMBED_WIDTH).astype(jnp.float32)
    negative_rows = right_part[negative].astype(jnp.float32)
    score_matrix = jnp.einsum('wet,wjt->wej', query_block_rows, negative_rows)
    positive_score_grad = -jax.nn.sigmoid(-positive)
    negative_score_grad = (NEG_WEIGHT * jax.nn.sigmoid(score_matrix)).astype(jnp.bfloat16).astype(jnp.float32)
    query_gradient = positive_score_grad[:, None] * target_embedding + jnp.einsum('fjs,fsh->fjh', negative_score_grad, negative_rows).reshape(-1, EMBED_WIDTH)
    negative_embedding_grad = jnp.einsum('fre,frl->fel', negative_score_grad, query_block_rows).astype(jnp.bfloat16)
    target_grad = (positive_score_grad[:, None] * query).astype(jnp.bfloat16)
    source_grad = complex_back(query_gradient, relation_emb).astype(jnp.bfloat16)
    relation_grad = complex_back(query_gradient, source_emb).astype(jnp.bfloat16)
    left_term = jnp.zeros((left_part.shape[0], EMBED_WIDTH), jnp.float32).at[source].add(source_grad.astype(jnp.float32))
    all_ids = jnp.concatenate([target, negative.reshape(-1)])
    all_grads = jnp.concatenate([target_grad, negative_embedding_grad.reshape(-1, EMBED_WIDTH)], axis=0).astype(jnp.float32)
    right_term = jnp.zeros((right_part.shape[0], EMBED_WIDTH), jnp.float32).at[all_ids].add(all_grads)
    relation_term = jnp.zeros((NREL, EMBED_WIDTH), jnp.float32).at[relation].add(relation_grad.astype(jnp.float32))
    return (left_term, right_term, relation_term)

def adagrad(table, state, grad):
    state_new = state + lax.optimization_barrier(jnp.mean(grad * grad, axis=-1))
    return (table - LEARN_RATE * grad / jnp.sqrt(state_new)[:, None], state_new)

def reference(left_table, left_state, right_table, right_state, relation_table, relation_state, source_ids, target_ids, relation_ids, negative_ids):
    left_bf = left_table.astype(jnp.bfloat16).reshape(N_LEFT, N_RIGHT * ROWS, EMBED_WIDTH)
    right_bf = right_table.astype(jnp.bfloat16).reshape(N_LEFT, N_RIGHT, ROWS, EMBED_WIDTH)
    right_bf = right_bf.transpose(1, 0, 2, 3).reshape(N_RIGHT, N_LEFT * ROWS, EMBED_WIDTH)
    relation_bf = relation_table.astype(jnp.bfloat16)

    def visit(carry, index):
        left_acc, right_acc, relation_acc = carry
        row_index = index // N_RIGHT
        column = index % N_RIGHT
        partner = (column + N_RIGHT - 1) % N_RIGHT
        terms = bucket_grads(left_bf[row_index], right_bf[partner], relation_bf, source_ids[row_index, column], target_ids[row_index, column], relation_ids[row_index, column], negative_ids[row_index, column])
        return ((left_acc.at[row_index].add(terms[0]), right_acc.at[partner].add(terms[1]), relation_acc + terms[2]), None)
    start_carry = (jnp.zeros((N_LEFT, N_RIGHT * ROWS, EMBED_WIDTH), jnp.float32), jnp.zeros((N_RIGHT, N_LEFT * ROWS, EMBED_WIDTH), jnp.float32), jnp.zeros((NREL, EMBED_WIDTH), jnp.float32))
    (left_grad, right_grad, relation_grad), _ = lax.scan(visit, start_carry, jnp.arange(N_LEFT * N_RIGHT, dtype=jnp.int32))
    left_new, left_state_new = adagrad(left_table, left_state, left_grad.reshape(-1, EMBED_WIDTH))
    right_grad = right_grad.reshape(N_RIGHT, N_LEFT, ROWS, EMBED_WIDTH).transpose(1, 0, 2, 3).reshape(-1, EMBED_WIDTH)
    right_upd, right_state_upd = adagrad(right_table, right_state, right_grad)
    right_new = jnp.roll(right_upd.reshape(N_LEFT, N_RIGHT, ROWS, EMBED_WIDTH), 1, axis=1).reshape(-1, EMBED_WIDTH)
    right_state_new = jnp.roll(right_state_upd.reshape(N_LEFT, N_RIGHT, ROWS), 1, axis=1).reshape(-1)
    relation_new, relation_state_new = adagrad(relation_table, relation_state, relation_grad)
    return (left_new, left_state_new, right_new, right_state_new, relation_new, relation_state_new)
```

```python
import functools

import jax
import jax.numpy as jnp
from jax import lax
from jax.experimental import pallas as pl
from jax.experimental.pallas import tpu as pltpu
from jax.sharding import PartitionSpec as P

LEARN_RATE = 0.1
NEG_WEIGHT = 0.03125
MESH = pl.DeviceIdType.MESH
F32, BF16 = jnp.float32, jnp.bfloat16

N = 16
W = 400
HALF = 200
B = 128
LOW = 208
HIGH = W - LOW
VMEM_LIMIT = 60 * 1024 * 1024


def mod(value, n):
    return lax.rem(value + 4 * n, n)


class Place:
    def __init__(self):
        self.l = lax.axis_index("left")
        self.r = lax.axis_index("right")
        self.z = lax.div(self.l, 2)
        self.h = lax.rem(self.l, 2)
        self.c = lax.rem(self.r, 2)
        self.x = lax.rem(lax.div(self.r, 2), 4)
        self.yl = lax.div(self.r, 8)

    def left_at(self, z, k=0):
        h = self.h if k == 0 else 1 - self.h
        return mod(self.z + z, 8) * 2 + h

    def right_at(self, x, k=0, other=0):
        yl = self.yl if k == 0 else 1 - self.yl
        c = self.c if other == 0 else 1 - self.c
        return (yl * 4 + mod(self.x + x, 4)) * 2 + c


def remote(src, dst, send, recv, left, right):
    return pltpu.make_async_remote_copy(
        src_ref=src,
        dst_ref=dst,
        send_sem=send,
        recv_sem=recv,
        device_id=(left, right),
        device_id_type=MESH,
    )


def greet(peers):
    barrier = pltpu.get_barrier_semaphore()
    for left, right in peers:
        pl.semaphore_signal(barrier, inc=1, device_id=(left, right), device_id_type=MESH)
    pl.semaphore_wait(barrier, len(peers))


def gather_kernel(lt, rt, table, state, lg, rg, moved, moved_state, ss, rs, ls, lr, ms):
    me = Place()
    l, r = me.l, me.r
    ahead, behind = mod(r + 1, N), mod(r - 1, N)
    l_other = me.left_at(0, 1)
    zp, zm = me.left_at(1), me.left_at(-1)
    xp, xm = me.right_at(1), me.right_at(-1)
    yo, co = me.right_at(0, 1), me.right_at(0, 0, 1)
    barrier = pltpu.get_barrier_semaphore()
    to = [(l, ahead), (l_other, ahead), (l, behind), (l_other, behind), (zp, r), (zm, r)]
    to += [(l, xp), (l, xm), (l, yo), (l, co)]
    for a, b in to:
        pl.semaphore_signal(barrier, inc=1, device_id=(a, b), device_id_type=MESH)
    own = pltpu.make_async_copy(lt, lg.at[r], ms.at[4])
    own.start()
    pl.semaphore_wait(barrier, len(to))

    sends = []

    def send(src, dst, s, d, left, right):
        copy = remote(src, dst, s, d, left, right)
        copy.start()
        sends.append(copy)

    def arrived(dst, d):
        remote(dst, dst, ms.at[5], d, l, co).wait_recv()

    send(rt, rg.at[l], ss.at[0], rs.at[0], l, ahead)
    send(rt, rg.at[l], ss.at[1], rs.at[1], l_other, ahead)
    send(lt, lg.at[r], ls.at[0], lr.at[0], l, yo)
    send(lt, lg.at[r], ls.at[1], lr.at[1], l, xp)
    send(lt, lg.at[r], ls.at[2], lr.at[2], l, xm)
    send(lt, lg.at[r], ls.at[3], lr.at[3], l, co)

    lslot = lambda x, k=0: me.right_at(x, k)
    slot = lambda z, k: me.left_at(z, k)

    arrived(rg.at[l], rs.at[0])
    send(rg.at[l], rg.at[l], ss.at[2], rs.at[2], zp, r)
    send(rg.at[l], rg.at[l], ss.at[3], rs.at[3], zm, r)
    arrived(lg.at[yo], lr.at[0])
    send(lg.at[yo], lg.at[yo], ls.at[4], lr.at[4], l, xp)
    send(lg.at[yo], lg.at[yo], ls.at[5], lr.at[5], l, xm)
    send(lg.at[yo], lg.at[yo], ls.at[6], lr.at[6], l, co)
    arrived(rg.at[l_other], rs.at[1])
    send(rg.at[l_other], rg.at[l_other], ss.at[4], rs.at[4], zp, r)
    send(rg.at[l_other], rg.at[l_other], ss.at[5], rs.at[5], zm, r)
    send(table, moved, ms.at[0], ms.at[1], l, ahead)
    send(state, moved_state, ms.at[2], ms.at[3], l, ahead)

    def ring(d, k):
        i = 2 + 4 * (d - 1) + 2 * k
        a, b = slot(-d, k), slot(d, k)
        n = 6 + 4 * (d - 1) + 2 * k
        if d < 3:
            arrived(rg.at[a], rs.at[i])
            send(rg.at[a], rg.at[a], ss.at[n], rs.at[n], zp, r)
            arrived(rg.at[b], rs.at[i + 1])
            send(rg.at[b], rg.at[b], ss.at[n + 1], rs.at[n + 1], zm, r)
        else:
            low, high = pl.ds(0, LOW), pl.ds(LOW, HIGH)
            arrived(rg.at[a], rs.at[i])
            send(rg.at[a, low], rg.at[a, low], ss.at[n], rs.at[n], zp, r)
            arrived(rg.at[b], rs.at[i + 1])
            send(rg.at[b, high], rg.at[b, high], ss.at[n + 1], rs.at[n + 1], zm, r)

    def across(k):
        a, b = lslot(-1, k), lslot(1, k)
        ra, rb = (1, 2) if k == 0 else (4, 5)
        i = 7 + 4 * k
        low, high = pl.ds(0, LOW), pl.ds(LOW, HIGH)
        arrived(lg.at[a], lr.at[ra])
        send(lg.at[a, low], lg.at[a, low], ls.at[i], lr.at[i], l, xp)
        send(lg.at[a], lg.at[a], ls.at[i + 2], lr.at[i + 2], l, co)
        arrived(lg.at[b], lr.at[rb])
        send(lg.at[b, high], lg.at[b, high], ls.at[i + 1], lr.at[i + 1], l, xm)
        send(lg.at[b], lg.at[b], ls.at[i + 3], lr.at[i + 3], l, co)

    def far(k):
        a = lslot(2, k)
        i = 7 + 4 * k
        arrived(lg.at[a, pl.ds(0, LOW)], lr.at[i])
        arrived(lg.at[a, pl.ds(LOW, HIGH)], lr.at[i + 1])
        send(lg.at[a], lg.at[a], ls.at[15 + k], lr.at[15 + k], l, co)

    across(0)
    ring(1, 0)
    across(1)
    ring(1, 1)
    ring(2, 0)
    far(0)
    ring(2, 1)
    far(1)
    ring(3, 0)
    ring(3, 1)
    for x, k, i in ((0, 0, 3), (0, 1, 6), (-1, 0, 9), (1, 0, 10), (-1, 1, 13), (1, 1, 14), (2, 0, 15), (2, 1, 16)):
        arrived(lg.at[me.right_at(x, k, 1)], lr.at[i])
    for k in (0, 1):
        a = slot(4, k)
        arrived(rg.at[a, pl.ds(0, LOW)], rs.at[14 + 2 * k])
        arrived(rg.at[a, pl.ds(LOW, HIGH)], rs.at[15 + 2 * k])
    arrived(moved, ms.at[1])
    arrived(moved_state, ms.at[3])
    own.wait()
    for copy in sends:
        copy.wait_send()


def gather(lt, rt, table, state):
    vm = pl.BlockSpec(memory_space=pltpu.VMEM)
    return pl.pallas_call(
        gather_kernel,
        out_shape=(
            jax.ShapeDtypeStruct((N, W, B), BF16),
            jax.ShapeDtypeStruct((N, W, B), BF16),
            jax.ShapeDtypeStruct((B, W), F32),
            jax.ShapeDtypeStruct((1, B), F32),
        ),
        in_specs=[vm] * 4,
        out_specs=(vm,) * 4,
        scratch_shapes=[
            pltpu.SemaphoreType.DMA((18,)),
            pltpu.SemaphoreType.DMA((18,)),
            pltpu.SemaphoreType.DMA((17,)),
            pltpu.SemaphoreType.DMA((17,)),
            pltpu.SemaphoreType.DMA((6,)),
        ],
        compiler_params=pltpu.CompilerParams(collective_id=0, has_side_effects=True, vmem_limit_bytes=VMEM_LIMIT),
        name="gather_parts",
    )(lt, rt, table, state)


T = 256
STEPS = 4
J = 256
JS = 8


def one_hot(ids, first, rows):
    row = lax.broadcasted_iota(jnp.int32, (rows, ids.shape[-1]), 0) + first
    return row == ids


def back(g, o):
    g_re, g_im, o_re, o_im = g[:HALF], g[HALF:], o[:HALF], o[HALF:]
    return jnp.concatenate([g_re * o_re + g_im * o_im, g_im * o_re - g_re * o_im], axis=0)


def dot(a, b):
    return lax.dot_general(a, b, (((1,), (0,)), ((), ())), preferred_element_type=F32)


def dot_nt(a, b):
    return lax.dot_general(a, b, (((1,), (1,)), ((), ())), preferred_element_type=F32)


def bucket_kernel(lg, rg, rel, src, rid, tgt, neg, lout, rout, pout, rn, ohs, ohr, w, qs, sg, og, mult):
    for i in range(N):
        rn[pl.ds(i * B, B), :] = rg[i].T
    for j in range(JS):
        for c in range(2):
            hit = jnp.where(one_hot(neg[c], j * J, J), 1.0, 0.0)
            count = jnp.sum(hit, axis=1, keepdims=True) * NEG_WEIGHT
            mult[c, pl.ds(j * J, J), :] = jnp.broadcast_to(count, (J, B))
    lcat = lambda: jnp.concatenate([lg[i] for i in range(N)], axis=1)
    rcat = lambda: jnp.concatenate([rg[i] for i in range(N)], axis=1)

    def step(t, _):
        c = lax.div(t, 2)
        for j in range(JS):
            ohs[t, pl.ds(j * J, J), :] = jnp.where(one_hot(src[t], j * J, J), 1.0, 0.0).astype(BF16)
        ohr[t] = jnp.where(one_hot(rid[t], 0, 256), 1.0, 0.0).astype(BF16)
        s = dot(lcat(), ohs[t])
        o = dot(rel[...], ohr[t])
        s_re, s_im, o_re, o_im = s[:HALF], s[HALF:], o[:HALF], o[HALF:]
        q = jnp.concatenate([s_re * o_re - s_im * o_im, s_re * o_im + s_im * o_re], axis=0).astype(BF16)
        qs[t] = q
        positive = jnp.zeros((1, T), F32)
        for j in range(JS):
            score = dot(rn[pl.ds(j * J, J), :], q)
            hit = one_hot(tgt[t], j * J, J)
            positive += jnp.sum(jnp.where(hit, score, 0.0), axis=0, keepdims=True)
            m = mult[c, pl.ds(j * J, J), :]
            m = jnp.concatenate([m, m], axis=1)
            w[t, pl.ds(j * J, J), :] = (jax.nn.sigmoid(score) * m).astype(BF16)
        pos_grad = -jax.nn.sigmoid(-positive)
        for j in range(JS):
            hit = one_hot(tgt[t], j * J, J)
            old = w[t, pl.ds(j * J, J), :].astype(F32)
            w[t, pl.ds(j * J, J), :] = (old + jnp.where(hit, pos_grad, 0.0)).astype(BF16)
        g = dot(rcat(), w[t])
        sg[t] = back(g, o).astype(BF16)
        og[t] = back(g, s).astype(BF16)
        return 0

    lax.fori_loop(0, STEPS, step, 0)
    cat = lambda ref: jnp.concatenate([ref[t] for t in range(STEPS)], axis=1)
    rows = lambda ref, j: jnp.concatenate([ref[t, pl.ds(j * J, J), :] for t in range(STEPS)], axis=1)
    for j in range(JS):
        part = dot_nt(cat(qs), rows(w, j)).astype(BF16)
        rout[2 * j], rout[2 * j + 1] = part[:, :B], part[:, B:]
    for j in range(JS):
        part = dot_nt(cat(sg), rows(ohs, j)).astype(BF16)
        lout[2 * j], lout[2 * j + 1] = part[:, :B], part[:, B:]
    part = dot_nt(cat(ohr), cat(og)).astype(BF16)
    for i in range(N):
        pout[i] = part[i * 16 : i * 16 + 16]


def bucket(lg, rg, rel, src, rid, tgt, neg):
    vm = pl.BlockSpec(memory_space=pltpu.VMEM)
    return pl.pallas_call(
        bucket_kernel,
        out_shape=(
            jax.ShapeDtypeStruct((N, W, B), BF16),
            jax.ShapeDtypeStruct((N, W, B), BF16),
            jax.ShapeDtypeStruct((N, 16, W), BF16),
        ),
        in_specs=[vm] * 7,
        out_specs=(vm,) * 3,
        scratch_shapes=[
            pltpu.VMEM((N * B, W), BF16),
            pltpu.VMEM((STEPS, N * B, T), BF16),
            pltpu.VMEM((STEPS, 256, T), BF16),
            pltpu.VMEM((STEPS, N * B, T), BF16),
            pltpu.VMEM((STEPS, W, T), BF16),
            pltpu.VMEM((STEPS, W, T), BF16),
            pltpu.VMEM((STEPS, W, T), BF16),
            pltpu.VMEM((2, N * B, B), F32),
        ],
        compiler_params=pltpu.CompilerParams(vmem_limit_bytes=VMEM_LIMIT),
        name="bucket_grads",
    )(lg, rg, rel, src, rid, tgt, neg)


def scatter_kernel(
    lp, rp, pp, lsum, rsum, psum,
    rb_half, rb, rstage, ybuf, cbuf, lb_half, lb, lstage, lx, lybuf,
    pbuf, prow, qbuf, qrow, fbuf, fown,
    zs, zr, cs, cr, xs, xr, ps, pr, qs, qr, fs, fr, ts, tr,
):
    me = Place()
    l, r = me.l, me.r
    zp, zm = me.left_at(1), me.left_at(-1)
    xp, xm = me.right_at(1), me.right_at(-1)
    yo, co = me.right_at(0, 1), me.right_at(0, 0, 1)
    l_other = me.left_at(0, 1)
    barrier = pltpu.get_barrier_semaphore()
    for i in range(1, N):
        pl.semaphore_signal(barrier, inc=1, device_id=(l, mod(r + i, N)), device_id_type=MESH)
        pl.semaphore_signal(barrier, inc=1, device_id=(mod(l + i, N), r), device_id_type=MESH)
    pl.semaphore_wait(barrier, 2 * (N - 1))

    sends = []

    def send(src, dst, s, d, left, right):
        copy = remote(src, dst, s, d, left, right)
        copy.start()
        sends.append(copy)

    def arrived(dst, d):
        remote(dst, dst, ts.at[2], d, l, co).wait_recv()

    low, high = pl.ds(0, LOW), pl.ds(LOW, HIGH)
    part = (low, high)
    zto, xto, sign = (zp, zm), (xp, xm), (1, -1)

    for k in (1, 0):
        a = me.left_at(4, k)
        for side in (0, 1):
            rows = pl.ds(0, LOW if side == 0 else HIGH)
            send(rp.at[a, part[side]], rb_half.at[side, k, rows], zs.at[side, 3, k], zr.at[side, 3, k], zto[side], r)
    for n, (x, k) in enumerate(((2, 0), (2, 1), (1, 0), (-1, 0), (1, 1), (-1, 1), (0, 0), (0, 1))):
        send(lp.at[me.right_at(x, k, 1)], cbuf.at[n], cs.at[n], cr.at[n], l, co)
    for i in range(1, N):
        to = mod(r + i, N)
        send(pp.at[to], pbuf.at[i], ps.at[i], pr.at[i], l, to)

    def chip_sum(n, x, k):
        arrived(cbuf.at[n], cr.at[n])
        return lp[me.right_at(x, k)].astype(F32) + cbuf[n].astype(F32)

    def right_step(d, k):
        a, b = me.left_at(d, k), me.left_at(-d, k)
        for side, at in ((0, a), (1, b)):
            mine = rp[at].astype(F32)
            if d == 3:
                rows = pl.ds(0, LOW if side == 0 else HIGH)
                arrived(rb_half.at[side, k, rows], zr.at[side, 3, k])
                got = rb_half[side, k, rows].astype(F32)
                if side == 0:
                    total = jnp.concatenate([mine[:LOW] + got, mine[LOW:]], axis=0)
                else:
                    total = jnp.concatenate([mine[:LOW], mine[LOW:] + got], axis=0)
            else:
                arrived(rb.at[side, d, k], zr.at[side, d, k])
                total = mine + rb[side, d, k].astype(F32)
            rstage[side, d - 1, k] = total.astype(BF16)
            send(rstage.at[side, d - 1, k], rb.at[side, d - 1, k], zs.at[side, d - 1, k], zr.at[side, d - 1, k], zto[side], r)

    for k in (1, 0):
        total = chip_sum(0 if k == 0 else 1, 2, k).astype(BF16)
        lstage[0, k] = total
        for side in (0, 1):
            rows = pl.ds(0, LOW if side == 0 else HIGH)
            send(lstage.at[0, k, part[side]], lb_half.at[side, k, rows], xs.at[side, 1, k], xr.at[side, 1, k], l, xto[side])
    right_step(3, 1)
    right_step(3, 0)

    total = pp[r].astype(F32)
    for i in range(1, N):
        arrived(pbuf.at[i], pr.at[i])
        total += pbuf[i].astype(F32)
    for i in range(N):
        prow[i] = total[i : i + 1]
    for i in range(1, N):
        to = mod(l + i, N)
        send(prow.at[to], qbuf.at[i], qs.at[i], qr.at[i], to, r)

    for k in (1, 0):
        for side in (0, 1):
            n = 2 + 2 * k + side
            total = chip_sum(n, sign[side], k)
            rows = pl.ds(0, LOW if side == 0 else HIGH)
            arrived(lb_half.at[side, k, rows], xr.at[side, 1, k])
            got = lb_half[side, k, rows].astype(F32)
            if side == 0:
                total = jnp.concatenate([total[:LOW] + got, total[LOW:]], axis=0)
            else:
                total = jnp.concatenate([total[:LOW], total[LOW:] + got], axis=0)
            lstage[1 + side, k] = total.astype(BF16)
            send(lstage.at[1 + side, k], lb.at[side, k], xs.at[side, 0, k], xr.at[side, 0, k], l, xto[side])
    right_step(2, 1)
    right_step(2, 0)

    total = prow[l]
    for i in range(1, N):
        arrived(qbuf.at[i], qr.at[i])
        total += qbuf[i]
    qrow[l] = total
    for i in range(1, N):
        to = mod(l + i, N)
        send(qrow.at[l], qrow.at[l], fs.at[i], fr.at[i], to, r)

    other = chip_sum(7, 0, 1)
    for side in (0, 1):
        arrived(lb.at[side, 1], xr.at[side, 0, 1])
        other += lb[side, 1].astype(F32)
    lx[...] = other.astype(BF16)
    send(lx, lybuf, ts.at[0], tr.at[0], l, yo)
    right_step(1, 1)
    total = chip_sum(6, 0, 0)
    for side in (0, 1):
        arrived(lb.at[side, 0], xr.at[side, 0, 0])
        total += lb[side, 0].astype(F32)
    lsum[...] = total
    right_step(1, 0)

    for i in range(1, N):
        arrived(qrow.at[mod(l - i, N)], fr.at[i])
    fown[...] = jnp.concatenate([qrow[i] for i in range(N)], axis=0)
    psum[r] = fown[...]
    for i in range(1, N):
        to = mod(r + i, N)
        send(fown, fbuf.at[i], pbs(ps, i), pbs(pr, i), l, to)

    other = rp[me.left_at(0, 1)].astype(F32)
    for side in (0, 1):
        arrived(rb.at[side, 0, 1], zr.at[side, 0, 1])
        other += rb[side, 0, 1].astype(F32)
    ybuf[0] = other.astype(BF16)
    send(ybuf.at[0], ybuf.at[1], ts.at[1], tr.at[1], l_other, r)
    arrived(lybuf, tr.at[0])
    lsum[...] += lybuf[...].astype(F32)
    total = rp[l].astype(F32)
    for side in (0, 1):
        arrived(rb.at[side, 0, 0], zr.at[side, 0, 0])
        total += rb[side, 0, 0].astype(F32)
    for i in range(1, N):
        arrived(fbuf.at[i], pbs(pr, i))
        psum[mod(r - i, N)] = fbuf[i]
    arrived(ybuf.at[1], tr.at[1])
    rsum[...] = total + ybuf[1].astype(F32)
    for copy in sends:
        copy.wait_send()


def pbs(ref, i):
    return ref.at[N + i]


def scatter(lp, rp, pp):
    vm = pl.BlockSpec(memory_space=pltpu.VMEM)
    dma = pltpu.SemaphoreType.DMA
    return pl.pallas_call(
        scatter_kernel,
        out_shape=(
            jax.ShapeDtypeStruct((W, B), F32),
            jax.ShapeDtypeStruct((W, B), F32),
            jax.ShapeDtypeStruct((N, 16, W), F32),
        ),
        in_specs=[vm] * 3,
        out_specs=(vm,) * 3,
        scratch_shapes=[
            pltpu.VMEM((2, 2, LOW, B), BF16),
            pltpu.VMEM((2, 3, 2, W, B), BF16),
            pltpu.VMEM((2, 3, 2, W, B), BF16),
            pltpu.VMEM((2, W, B), BF16),
            pltpu.VMEM((8, W, B), BF16),
            pltpu.VMEM((2, 2, LOW, B), BF16),
            pltpu.VMEM((2, 2, W, B), BF16),
            pltpu.VMEM((3, 2, W, B), BF16),
            pltpu.VMEM((W, B), BF16),
            pltpu.VMEM((W, B), BF16),
            pltpu.VMEM((N, 16, W), BF16),
            pltpu.VMEM((N, 1, W), F32),
            pltpu.VMEM((N, 1, W), F32),
            pltpu.VMEM((N, 1, W), F32),
            pltpu.VMEM((N, 16, W), F32),
            pltpu.VMEM((16, W), F32),
            dma((2, 4, 2)), dma((2, 4, 2)),
            dma((8,)), dma((8,)),
            dma((2, 2, 2)), dma((2, 2, 2)),
            dma((2 * N,)), dma((2 * N,)),
            dma((N,)), dma((N,)),
            dma((N,)), dma((N,)),
            dma((3,)), dma((2,)),
        ],
        compiler_params=pltpu.CompilerParams(collective_id=1, has_side_effects=True, vmem_limit_bytes=VMEM_LIMIT),
        name="scatter_grads",
    )(lp, rp, pp)


def adagrad(table, state, grad):
    state_new = state + jnp.mean(grad * grad, axis=-1)
    return (table - LEARN_RATE * grad / jnp.sqrt(state_new)[:, None], state_new)


def per_device(
    left_table,
    left_state,
    right_table,
    right_state,
    relation_table,
    relation_state,
    source_ids,
    target_ids,
    relation_ids,
    negative_ids,
):
    lt = left_table.astype(BF16).T
    rt = right_table.astype(BF16).T
    lg, rg, moved_table, moved_state = gather(lt, rt, right_table, right_state.reshape(1, B))
    rel = relation_table.astype(BF16).T
    src = source_ids.reshape(STEPS, 1, T)
    rid = relation_ids.reshape(STEPS, 1, T)
    tgt = target_ids.reshape(STEPS, 1, T)
    neg = negative_ids.reshape(2, 1, 1024)
    lp, rp, pp = bucket(lg, rg, rel, src, rid, tgt, neg)
    lsum, rsum, psum = scatter(lp, rp, pp)
    left_new, left_state_new = adagrad(left_table, left_state, lsum.T)
    right_new, right_state_new = adagrad(moved_table, moved_state.reshape(B), rsum.T)
    relation_new, relation_state_new = adagrad(relation_table, relation_state, psum.reshape(N * 16, W))
    return (left_new, left_state_new, right_new, right_state_new, relation_new, relation_state_new)


def solution(mesh):
    return jax.shard_map(
        per_device,
        mesh=mesh,
        in_specs=(
            P(("left", "right"), None),
            P(("left", "right")),
            P(("left", "right"), None),
            P(("left", "right")),
            P(),
            P(),
            P("left", "right", None),
            P("left", "right", None),
            P("left", "right", None),
            P("left", "right", None, None),
        ),
        out_specs=(
            P(("left", "right"), None),
            P(("left", "right")),
            P(("left", "right"), None),
            P(("left", "right")),
            P(),
            P(),
        ),
        check_vma=False,
    )
```

```python
import functools

import jax
import jax.numpy as jnp
from jax import lax
from jax.experimental import pallas as pl
from jax.experimental.pallas import tpu as pltpu
from jax.sharding import PartitionSpec as P

LEARN_RATE = 0.1
NEG_WEIGHT = 0.03125
MESH = pl.DeviceIdType.MESH
F32, BF16 = jnp.float32, jnp.bfloat16

N = 16
W = 400
HALF = 200
B = 128
LOW = 208
HIGH = W - LOW
VMEM_LIMIT = 60 * 1024 * 1024


def mod(value, n):
    return lax.rem(value + 4 * n, n)


class Place:
    def __init__(self):
        self.l = lax.axis_index("left")
        self.r = lax.axis_index("right")
        self.z = lax.div(self.l, 2)
        self.h = lax.rem(self.l, 2)
        self.c = lax.rem(self.r, 2)
        self.x = lax.rem(lax.div(self.r, 2), 4)
        self.yl = lax.div(self.r, 8)

    def left_at(self, z, k=0):
        h = self.h if k == 0 else 1 - self.h
        return mod(self.z + z, 8) * 2 + h

    def right_at(self, x, k=0, other=0):
        yl = self.yl if k == 0 else 1 - self.yl
        c = self.c if other == 0 else 1 - self.c
        return (yl * 4 + mod(self.x + x, 4)) * 2 + c


def remote(src, dst, send, recv, left, right):
    return pltpu.make_async_remote_copy(
        src_ref=src,
        dst_ref=dst,
        send_sem=send,
        recv_sem=recv,
        device_id=(left, right),
        device_id_type=MESH,
    )


E = 1024
T = 256
TILES = tuple(slice(t * T, t * T + T) for t in range(E // T))
J = 256
LOWS, HIGHS = pl.ds(0, LOW), pl.ds(LOW, HIGH)
PART = (LOWS, HIGHS)


def one_hot(ids, first, rows):
    row = lax.broadcasted_iota(jnp.int32, (rows, ids.shape[-1]), 0)
    return row == ids - first


def ones(hit):
    return jnp.where(hit, 1.0, 0.0).astype(BF16)


def back(g, o):
    g_re, g_im, o_re, o_im = g[:HALF], g[HALF:], o[:HALF], o[HALF:]
    return jnp.concatenate([g_re * o_re + g_im * o_im, g_im * o_re - g_re * o_im], axis=0)


def dot(a, b):
    return lax.dot_general(a, b, (((1,), (0,)), ((), ())), preferred_element_type=F32)


def dot_nt(a, b):
    return lax.dot_general(a, b, (((1,), (1,)), ((), ())), preferred_element_type=F32)


def bucket_kernel(
    left, right, state, relation, src, rid, tgt, neg,
    lsum, rsum, psum, moved, moved_state,
    lt, rt, lg, rg, rn, rel, ohs, ohr, w, qs, ss_, os_, sg, og, mult, pos,
    rp, lp, pp,
    rb_half, rb, rstage, rfar, ybuf, cst, cbuf, lb_half, lb, lstage, lx, lybuf,
    pbuf, prow, qbuf, qrow, fbuf, fown,
    gs, gr, ls, lr, ms,
    zs, zr, cs, cr, xs, xr, ps, pr, qsm, qrm, fs, fr, ts, tr,
):
    me = Place()
    l, r = me.l, me.r
    ahead, behind = mod(r + 1, N), mod(r - 1, N)
    l_other = me.left_at(0, 1)
    zp, zm = me.left_at(1), me.left_at(-1)
    xp, xm = me.right_at(1), me.right_at(-1)
    yo, co = me.right_at(0, 1), me.right_at(0, 0, 1)
    barrier = pltpu.get_barrier_semaphore()

    def greet(a, b):
        pl.semaphore_signal(barrier, inc=1, device_id=(a, b), device_id_type=MESH)

    for i in range(1, N):
        greet(l, mod(r + i, N))
        greet(mod(l + i, N), r)
    greet(l_other, ahead)
    greet(l_other, behind)

    sends = []

    def send(src_ref, dst, s, d, a, b):
        copy = remote(src_ref, dst, s, d, a, b)
        copy.start()
        sends.append(copy)

    def arrived(dst, d):
        remote(dst, dst, ts.at[2], d, l, co).wait_recv()

    rt[...] = right[...].T.astype(BF16)
    lt[...] = left[...].T.astype(BF16)
    lg[r] = lt[...]
    rel[...] = relation[...].T.astype(BF16)
    ids = lambda ref, t: ref[0, :, TILES[t]]

    def counts(c, j):
        hit = jnp.where(one_hot(neg[0, 0, c : c + 1, :], j * J, J), NEG_WEIGHT, 0.0)
        mult[c, pl.ds(j * J, J), :] = jnp.broadcast_to(jnp.sum(hit, axis=1, keepdims=True), (J, B))

    def source_hot(j):
        ohs[pl.ds(j * J, J), :] = ones(one_hot(src[0], j * J, J))

    ohr[...] = ones(one_hot(rid[0], 0, 256))
    pos[...] = jnp.zeros_like(pos)
    pl.semaphore_wait(barrier, 2 * (N - 1) + 2)

    send(rt, rg.at[l], gs.at[0], gr.at[0], l, ahead)
    send(rt, rg.at[l], gs.at[1], gr.at[1], l_other, ahead)
    send(lt, lg.at[r], ls.at[0], lr.at[0], l, yo)
    send(lt, lg.at[r], ls.at[1], lr.at[1], l, xp)
    send(lt, lg.at[r], ls.at[2], lr.at[2], l, xm)
    send(lt, lg.at[r], ls.at[3], lr.at[3], l, co)

    def ring(d, k):
        i = 2 + 4 * (d - 1) + 2 * k
        a, b = me.left_at(-d, k), me.left_at(d, k)
        n = i + 4
        arrived(rg.at[a], gr.at[i])
        up, down = (rg.at[a], rg.at[b]) if d < 3 else (rg.at[a, LOWS], rg.at[b, HIGHS])
        send(up, up, gs.at[n], gr.at[n], zp, r)
        arrived(rg.at[b], gr.at[i + 1])
        send(down, down, gs.at[n + 1], gr.at[n + 1], zm, r)

    def across(k):
        a, b = me.right_at(-1, k), me.right_at(1, k)
        ra, rb_ = (1, 2) if k == 0 else (4, 5)
        i = 7 + 4 * k
        arrived(lg.at[a], lr.at[ra])
        send(lg.at[a, LOWS], lg.at[a, LOWS], ls.at[i], lr.at[i], l, xp)
        send(lg.at[a], lg.at[a], ls.at[i + 2], lr.at[i + 2], l, co)
        arrived(lg.at[b], lr.at[rb_])
        send(lg.at[b, HIGHS], lg.at[b, HIGHS], ls.at[i + 1], lr.at[i + 1], l, xm)
        send(lg.at[b], lg.at[b], ls.at[i + 3], lr.at[i + 3], l, co)

    def far(k):
        a = me.right_at(2, k)
        i = 7 + 4 * k
        arrived(lg.at[a, LOWS], lr.at[i])
        arrived(lg.at[a, HIGHS], lr.at[i + 1])
        send(lg.at[a], lg.at[a], ls.at[15 + k], lr.at[15 + k], l, co)

    for j in range(5):
        counts(0, j)
    arrived(rg.at[l], gr.at[0])
    send(rg.at[l], rg.at[l], gs.at[2], gr.at[2], zp, r)
    send(rg.at[l], rg.at[l], gs.at[3], gr.at[3], zm, r)
    arrived(lg.at[yo], lr.at[0])
    send(lg.at[yo], lg.at[yo], ls.at[4], lr.at[4], l, xp)
    send(lg.at[yo], lg.at[yo], ls.at[5], lr.at[5], l, xm)
    send(lg.at[yo], lg.at[yo], ls.at[6], lr.at[6], l, co)
    across(0)
    for j in range(5, 8):
        counts(0, j)
    arrived(rg.at[l_other], gr.at[1])
    send(rg.at[l_other], rg.at[l_other], gs.at[4], gr.at[4], zp, r)
    send(rg.at[l_other], rg.at[l_other], gs.at[5], gr.at[5], zm, r)
    send(right, moved, ms.at[0], ms.at[1], l, ahead)
    send(state, moved_state, ms.at[2], ms.at[3], l, ahead)
    for j in range(2):
        counts(1, j)
    ring(1, 0)
    across(1)
    for j in range(2, 8):
        counts(1, j)
    far(0)
    ring(1, 1)
    for j in range(4):
        source_hot(j)
    far(1)
    for j in range(4, 8):
        source_hot(j)
    for t in range(4):
        os_[:, TILES[t]] = dot(rel[...], ohr[:, TILES[t]])
    ring(2, 0)
    for x, k, i in ((0, 0, 3), (0, 1, 6), (-1, 0, 9), (1, 0, 10), (-1, 1, 13), (1, 1, 14), (2, 0, 15), (2, 1, 16)):
        arrived(lg.at[me.right_at(x, k, 1)], lr.at[i])

    lcat = lambda: jnp.concatenate([lg[i] for i in range(N)], axis=1)
    rcat = lambda: jnp.concatenate([rg[i] for i in range(N)], axis=1)

    def queries(t):
        s = dot(lcat(), ohs[:, TILES[t]])
        o = os_[:, TILES[t]]
        ss_[:, TILES[t]] = s
        s_re, s_im, o_re, o_im = s[:HALF], s[HALF:], o[:HALF], o[HALF:]
        q = jnp.concatenate([s_re * o_re - s_im * o_im, s_re * o_im + s_im * o_re], axis=0)
        qs[:, TILES[t]] = q.astype(BF16)

    def rows_of(d):
        return pl.multiple_of(mod(me.z + d, 8) * J, J)

    def turn(d):
        zi = mod(me.z + d, 8)
        first = rows_of(d)
        rn[pl.ds(first, B), :] = rg[2 * zi].T
        rn[pl.ds(first + B, B), :] = rg[2 * zi + 1].T

    def scores(d):
        first = rows_of(d)
        for t in range(4):
            score = dot(rn[pl.ds(first, J), :], qs[:, TILES[t]])
            hit = one_hot(ids(tgt, t), first, J)
            found = jnp.where(hit, score, 0.0)
            pos[:, TILES[t]] += jnp.sum(found.reshape(J // 8, 8, T), axis=0)
            m = mult[t // 2, pl.ds(first, J), :]
            m = jnp.concatenate([m, m], axis=1)
            w[pl.ds(first, J), TILES[t]] = (jax.nn.sigmoid(score) * m).astype(BF16)

    turn(0)
    turn(1)
    turn(-1)
    queries(0)
    queries(1)
    ring(2, 1)
    queries(2)
    queries(3)
    scores(0)
    ring(3, 0)
    scores(1)
    scores(-1)
    turn(2)
    turn(-2)
    ring(3, 1)
    scores(2)
    scores(-2)
    turn(3)
    turn(-3)
    scores(3)
    scores(-3)
    for k in (0, 1):
        a = me.left_at(4, k)
        arrived(rg.at[a, LOWS], gr.at[14 + 2 * k])
        arrived(rg.at[a, HIGHS], gr.at[15 + 2 * k])
    turn(4)
    scores(4)

    def pos_grads(t):
        positive = jnp.sum(pos[:, TILES[t]], axis=0, keepdims=True)
        return -jax.nn.sigmoid(-positive)

    grads = [pos_grads(t) for t in range(4)]

    def weights(d):
        first = rows_of(d)
        for t in range(4):
            hit = one_hot(ids(tgt, t), first, J)
            old = w[pl.ds(first, J), TILES[t]].astype(F32)
            w[pl.ds(first, J), TILES[t]] = (old + jnp.where(hit, grads[t], 0.0)).astype(BF16)

    def right_grad(d):
        zi = mod(me.z + d, 8)
        part = dot_nt(qs[...], w[pl.ds(rows_of(d), J), :])
        rp[2 * zi] = part[:, :B]
        rp[2 * zi + 1] = part[:, B:]

    zto, xto, sign = (zp, zm), (xp, xm), (1, -1)

    weights(4)
    right_grad(4)
    for k in (1, 0):
        rfar[k] = rp[me.left_at(4, k)].astype(BF16)
    for k in (1, 0):
        for side in (0, 1):
            rows = pl.ds(0, LOW if side == 0 else HIGH)
            send(rfar.at[k, PART[side]], rb_half.at[side, k, rows], zs.at[side, 3, k], zr.at[side, 3, k], zto[side], r)
    weights(3)
    right_grad(3)
    weights(-3)
    right_grad(-3)
    for d in (2, -2, 1, -1, 0):
        weights(d)

    def right_step(d, k):
        for side, at in ((0, me.left_at(d, k)), (1, me.left_at(-d, k))):
            mine = rp[at]
            if d == 3:
                rows = pl.ds(0, LOW if side == 0 else HIGH)
                arrived(rb_half.at[side, k, rows], zr.at[side, 3, k])
                got = rb_half[side, k, rows].astype(F32)
                if side == 0:
                    total = jnp.concatenate([mine[:LOW] + got, mine[LOW:]], axis=0)
                else:
                    total = jnp.concatenate([mine[:LOW], mine[LOW:] + got], axis=0)
            else:
                arrived(rb.at[side, d, k], zr.at[side, d, k])
                total = mine + rb[side, d, k].astype(F32)
            rstage[side, d - 1, k] = total.astype(BF16)
            send(rstage.at[side, d - 1, k], rb.at[side, d - 1, k], zs.at[side, d - 1, k], zr.at[side, d - 1, k], zto[side], r)

    def query_grads(t):
        g = dot(rcat(), w[:, TILES[t]])
        sg[:, TILES[t]] = back(g, os_[:, TILES[t]]).astype(BF16)
        og[:, TILES[t]] = back(g, ss_[:, TILES[t]]).astype(BF16)

    query_grads(0)
    right_step(3, 1)
    right_step(3, 0)
    for t in range(1, 4):
        query_grads(t)
    part = dot_nt(ohr[...], og[...]).astype(BF16)
    for i in range(N):
        pp[i] = part[i * 16 : i * 16 + 16]
    for i in range(1, N):
        to = mod(r + i, N)
        send(pp.at[to], pbuf.at[i], ps.at[i], pr.at[i], l, to)
    right_grad(2)
    right_grad(-2)

    order = ((2, 0), (2, 1), (1, 0), (-1, 0), (1, 1), (-1, 1), (0, 0), (0, 1))

    def left_grad(n):
        x, k = order[n]
        g = lax.div(me.right_at(x, k), 2)
        part = dot_nt(sg[...], ohs[pl.ds(pl.multiple_of(g * J, J), J), :])
        lp[2 * g] = part[:, :B]
        lp[2 * g + 1] = part[:, B:]
        cst[n] = lp[me.right_at(x, k, 1)].astype(BF16)
        send(cst.at[n], cbuf.at[n], cs.at[n], cr.at[n], l, co)

    def chip_sum(n):
        x, k = order[n]
        arrived(cbuf.at[n], cr.at[n])
        return lp[me.right_at(x, k)] + cbuf[n].astype(F32)

    for n in range(6):
        left_grad(n)
    right_step(2, 1)
    right_step(2, 0)
    for k in (1, 0):
        lstage[0, k] = chip_sum(k).astype(BF16)
        for side in (0, 1):
            rows = pl.ds(0, LOW if side == 0 else HIGH)
            send(lstage.at[0, k, PART[side]], lb_half.at[side, k, rows], xs.at[side, 1, k], xr.at[side, 1, k], l, xto[side])
    left_grad(6)
    left_grad(7)
    right_grad(1)
    right_grad(-1)
    right_grad(0)

    total = pp[r].astype(F32)
    for i in range(1, N):
        arrived(pbuf.at[i], pr.at[i])
        total += pbuf[i].astype(F32)
    for i in range(N):
        prow[i] = total[i : i + 1]
    for i in range(1, N):
        to = mod(l + i, N)
        send(prow.at[to], qbuf.at[i], qsm.at[i], qrm.at[i], to, r)

    right_step(1, 1)
    for k in (1, 0):
        for side in (0, 1):
            total = chip_sum(2 + 2 * k + side)
            rows = pl.ds(0, LOW if side == 0 else HIGH)
            arrived(lb_half.at[side, k, rows], xr.at[side, 1, k])
            got = lb_half[side, k, rows].astype(F32)
            if side == 0:
                total = jnp.concatenate([total[:LOW] + got, total[LOW:]], axis=0)
            else:
                total = jnp.concatenate([total[:LOW], total[LOW:] + got], axis=0)
            lstage[1 + side, k] = total.astype(BF16)
            send(lstage.at[1 + side, k], lb.at[side, k], xs.at[side, 0, k], xr.at[side, 0, k], l, xto[side])
    right_step(1, 0)

    total = prow[l]
    for i in range(1, N):
        arrived(qbuf.at[i], qrm.at[i])
        total += qbuf[i]
    qrow[l] = total
    for i in range(1, N):
        to = mod(l + i, N)
        send(qrow.at[l], qrow.at[l], fs.at[i], fr.at[i], to, r)

    other = rp[me.left_at(0, 1)]
    for side in (0, 1):
        arrived(rb.at[side, 0, 1], zr.at[side, 0, 1])
        other += rb[side, 0, 1].astype(F32)
    ybuf[0] = other.astype(BF16)
    send(ybuf.at[0], ybuf.at[1], ts.at[1], tr.at[1], l_other, r)
    other = chip_sum(7)
    for side in (0, 1):
        arrived(lb.at[side, 1], xr.at[side, 0, 1])
        other += lb[side, 1].astype(F32)
    lx[...] = other.astype(BF16)
    send(lx, lybuf, ts.at[0], tr.at[0], l, yo)
    total = chip_sum(6)
    for side in (0, 1):
        arrived(lb.at[side, 0], xr.at[side, 0, 0])
        total += lb[side, 0].astype(F32)
    lsum[...] = total

    for i in range(1, N):
        arrived(qrow.at[mod(l - i, N)], fr.at[i])
    fown[...] = jnp.concatenate([qrow[i] for i in range(N)], axis=0)
    psum[r] = fown[...]
    for i in range(1, N):
        to = mod(r + i, N)
        send(fown, fbuf.at[i], ps.at[N + i], pr.at[N + i], l, to)

    total = rp[l]
    for side in (0, 1):
        arrived(rb.at[side, 0, 0], zr.at[side, 0, 0])
        total += rb[side, 0, 0].astype(F32)
    arrived(ybuf.at[1], tr.at[1])
    rsum[...] = total + ybuf[1].astype(F32)
    arrived(lybuf, tr.at[0])
    lsum[...] += lybuf[...].astype(F32)
    arrived(moved, ms.at[1])
    arrived(moved_state, ms.at[3])
    for i in range(1, N):
        arrived(fbuf.at[i], pr.at[N + i])
        psum[mod(r - i, N)] = fbuf[i]
    for copy in sends:
        copy.wait_send()


def bucket(left, right, state, relation, src, rid, tgt, neg):
    vm = pl.BlockSpec(memory_space=pltpu.VMEM)
    dma = pltpu.SemaphoreType.DMA
    blocks = pltpu.VMEM((N, W, B), BF16)
    return pl.pallas_call(
        bucket_kernel,
        out_shape=(
            jax.ShapeDtypeStruct((W, B), F32),
            jax.ShapeDtypeStruct((W, B), F32),
            jax.ShapeDtypeStruct((N, 16, W), F32),
            jax.ShapeDtypeStruct((B, W), F32),
            jax.ShapeDtypeStruct((1, B), F32),
        ),
        in_specs=[vm] * 8,
        out_specs=(vm,) * 5,
        scratch_shapes=[
            pltpu.VMEM((W, B), BF16),
            pltpu.VMEM((W, B), BF16),
            blocks,
            blocks,
            pltpu.VMEM((N * B, W), BF16),
            pltpu.VMEM((W, 256), BF16),
            pltpu.VMEM((N * B, E), BF16),
            pltpu.VMEM((256, E), BF16),
            pltpu.VMEM((N * B, E), BF16),
            pltpu.VMEM((W, E), BF16),
            pltpu.VMEM((W, E), F32),
            pltpu.VMEM((W, E), F32),
            pltpu.VMEM((W, E), BF16),
            pltpu.VMEM((W, E), BF16),
            pltpu.VMEM((2, N * B, B), F32),
            pltpu.VMEM((8, E), F32),
            pltpu.VMEM((N, W, B), F32),
            pltpu.VMEM((N, W, B), F32),
            pltpu.VMEM((N, 16, W), BF16),
            pltpu.VMEM((2, 2, LOW, B), BF16),
            pltpu.VMEM((2, 3, 2, W, B), BF16),
            pltpu.VMEM((2, 3, 2, W, B), BF16),
            pltpu.VMEM((2, W, B), BF16),
            pltpu.VMEM((2, W, B), BF16),
            pltpu.VMEM((8, W, B), BF16),
            pltpu.VMEM((8, W, B), BF16),
            pltpu.VMEM((2, 2, LOW, B), BF16),
            pltpu.VMEM((2, 2, W, B), BF16),
            pltpu.VMEM((3, 2, W, B), BF16),
            pltpu.VMEM((W, B), BF16),
            pltpu.VMEM((W, B), BF16),
            pltpu.VMEM((N, 16, W), BF16),
            pltpu.VMEM((N, 1, W), F32),
            pltpu.VMEM((N, 1, W), F32),
            pltpu.VMEM((N, 1, W), F32),
            pltpu.VMEM((N, 16, W), F32),
            pltpu.VMEM((16, W), F32),
            dma((18,)), dma((18,)), dma((17,)), dma((17,)), dma((4,)),
            dma((2, 4, 2)), dma((2, 4, 2)),
            dma((8,)), dma((8,)),
            dma((2, 2, 2)), dma((2, 2, 2)),
            dma((2 * N,)), dma((2 * N,)),
            dma((N,)), dma((N,)),
            dma((N,)), dma((N,)),
            dma((3,)), dma((2,)),
        ],
        compiler_params=pltpu.CompilerParams(collective_id=0, has_side_effects=True, vmem_limit_bytes=VMEM_LIMIT),
        name="bucket_round",
    )(left, right, state, relation, src, rid, tgt, neg)


def update_kernel(left, left_state, lsum, moved, moved_state, rsum, rel, rel_state, psum, lo, lso, ro, rso, po, pso):
    for table, state, grad, out, state_out in (
        (left, left_state, lsum, lo, lso),
        (moved, moved_state, rsum, ro, rso),
    ):
        g = grad[...]
        new = state[...] + jnp.sum(g * g, axis=0, keepdims=True) * (1.0 / W)
        state_out[...] = new
        out[...] = table[...] - (LEARN_RATE * g / jnp.sqrt(new)).T
    g = psum[...].reshape(256, W)
    mean = jnp.sum(g * g, axis=1, keepdims=True) * (1.0 / W)
    state = jnp.broadcast_to(rel_state[...], (8, 256)).T[:, :1]
    new = state + mean
    po[...] = rel[...] - LEARN_RATE * g / jnp.sqrt(new)
    pso[...] = jnp.broadcast_to(new, (256, 8)).T[:1]


def update(*args):
    vm = pl.BlockSpec(memory_space=pltpu.VMEM)
    return pl.pallas_call(
        update_kernel,
        out_shape=(
            jax.ShapeDtypeStruct((B, W), F32),
            jax.ShapeDtypeStruct((1, B), F32),
            jax.ShapeDtypeStruct((B, W), F32),
            jax.ShapeDtypeStruct((1, B), F32),
            jax.ShapeDtypeStruct((256, W), F32),
            jax.ShapeDtypeStruct((1, 256), F32),
        ),
        in_specs=[vm] * 9,
        out_specs=(vm,) * 6,
        name="update_tables",
    )(*args)


def per_device(
    left_table,
    left_state,
    right_table,
    right_state,
    relation_table,
    relation_state,
    source_ids,
    target_ids,
    relation_ids,
    negative_ids,
):
    row = lambda state: state.reshape(1, -1)
    lsum, rsum, psum, moved, moved_state = bucket(
        left_table, right_table, row(right_state), relation_table, source_ids, relation_ids, target_ids, negative_ids
    )
    left_new, left_state_new, right_new, right_state_new, relation_new, relation_state_new = update(
        left_table, row(left_state), lsum, moved, moved_state, rsum, relation_table, row(relation_state), psum
    )
    flat = lambda state: state.reshape(-1)
    return (left_new, flat(left_state_new), right_new, flat(right_state_new), relation_new, flat(relation_state_new))


def solution(mesh):
    return jax.shard_map(
        per_device,
        mesh=mesh,
        in_specs=(
            P(("left", "right"), None),
            P(("left", "right")),
            P(("left", "right"), None),
            P(("left", "right")),
            P(),
            P(),
            P("left", "right", None),
            P("left", "right", None),
            P("left", "right", None),
            P("left", "right", None, None),
        ),
        out_specs=(
            P(("left", "right"), None),
            P(("left", "right")),
            P(("left", "right"), None),
            P(("left", "right")),
            P(),
            P(),
        ),
        check_vma=False,
    )
```

```python
import functools

import jax
import jax.numpy as jnp
from jax import lax
from jax.experimental import pallas as pl
from jax.experimental.pallas import tpu as pltpu
from jax.sharding import PartitionSpec as P

LEARN_RATE = 0.1
NEG_WEIGHT = 0.03125
MESH = pl.DeviceIdType.MESH
F32, BF16 = jnp.float32, jnp.bfloat16

N = 16
W = 400
HALF = 200
B = 128
LOW = 208
HIGH = W - LOW
VMEM_LIMIT = 60 * 1024 * 1024


def mod(value, n):
    return lax.rem(value + 4 * n, n)


class Place:
    def __init__(self):
        self.l = lax.axis_index("left")
        self.r = lax.axis_index("right")
        self.z = lax.div(self.l, 2)
        self.h = lax.rem(self.l, 2)
        self.c = lax.rem(self.r, 2)
        self.x = lax.rem(lax.div(self.r, 2), 4)
        self.yl = lax.div(self.r, 8)

    def left_at(self, z, k=0):
        h = self.h if k == 0 else 1 - self.h
        return mod(self.z + z, 8) * 2 + h

    def right_at(self, x, k=0, other=0):
        yl = self.yl if k == 0 else 1 - self.yl
        c = self.c if other == 0 else 1 - self.c
        return (yl * 4 + mod(self.x + x, 4)) * 2 + c


def remote(src, dst, send, recv, left, right):
    return pltpu.make_async_remote_copy(
        src_ref=src,
        dst_ref=dst,
        send_sem=send,
        recv_sem=recv,
        device_id=(left, right),
        device_id_type=MESH,
    )


E = 1024
T = 256
TILES = tuple(slice(t * T, t * T + T) for t in range(E // T))
J = 256
LOWS, HIGHS = pl.ds(0, LOW), pl.ds(LOW, HIGH)
PART = (LOWS, HIGHS)


def one_hot(ids, first, rows):
    row = lax.broadcasted_iota(jnp.int32, (rows, ids.shape[-1]), 0)
    return row == ids - first


def ones(hit):
    return jnp.where(hit, 1.0, 0.0).astype(BF16)


def back(g, o):
    g_re, g_im, o_re, o_im = g[:HALF], g[HALF:], o[:HALF], o[HALF:]
    return jnp.concatenate([g_re * o_re + g_im * o_im, g_im * o_re - g_re * o_im], axis=0)


def dot(a, b):
    return lax.dot_general(a, b, (((1,), (0,)), ((), ())), preferred_element_type=F32)


def dot_nt(a, b):
    return lax.dot_general(a, b, (((1,), (1,)), ((), ())), preferred_element_type=F32)


def bucket_kernel(
    left, right, state, relation, src, rid, tgt, neg,
    lsum, rsum, psum, moved, moved_state,
    lt, rt, lg, rg, rn, rel, ohs, ohr, w, qs, ss_, os_, sg, og, mult,
    rp, lp, pp, oht, tt, gq, qf, tg,
    rb_half, rb, rstage, rfar, ybuf, cst, cbuf, lb_half, lb, lstage, lx, lybuf,
    pbuf, prow, qbuf, qrow, fbuf, fown,
    gs, gr, ls, lr, ms,
    zs, zr, cs, cr, xs, xr, ps, pr, qsm, qrm, fs, fr, ts, tr,
):
    me = Place()
    l, r = me.l, me.r
    ahead, behind = mod(r + 1, N), mod(r - 1, N)
    l_other = me.left_at(0, 1)
    zp, zm = me.left_at(1), me.left_at(-1)
    xp, xm = me.right_at(1), me.right_at(-1)
    yo, co = me.right_at(0, 1), me.right_at(0, 0, 1)
    barrier = pltpu.get_barrier_semaphore()

    def greet(a, b):
        pl.semaphore_signal(barrier, inc=1, device_id=(a, b), device_id_type=MESH)

    peers = [(a, b) for a in (l_other, zp, zm) for b in (ahead, behind)]
    peers += [(l, mod(r + i, N)) for i in range(1, N)] + [(mod(l + i, N), r) for i in range(1, N)]
    for a, b in peers:
        greet(a, b)

    sends = []

    def send(src_ref, dst, s, d, a, b):
        copy = remote(src_ref, dst, s, d, a, b)
        copy.start()
        sends.append(copy)

    def arrived(dst, d):
        remote(dst, dst, ts.at[2], d, l, co).wait_recv()

    rt[...] = right[...].astype(BF16)
    lt[...] = left[...].astype(BF16)
    lg[r] = lt[...]
    rel[...] = relation[...].astype(BF16)
    ids = lambda ref, t: ref[0, :, TILES[t]]

    def counts(c, j):
        hit = jnp.where(one_hot(neg[0, 0, c : c + 1, :], j * J, J), NEG_WEIGHT, 0.0)
        mult[c, pl.ds(j * J, J), :] = jnp.broadcast_to(jnp.sum(hit, axis=1, keepdims=True), (J, B))

    def source_hot(j):
        ohs[pl.ds(j * J, J), :] = ones(one_hot(src[0], j * J, J))
        oht[pl.ds(j * J, J), :] = ones(one_hot(tgt[0], j * J, J))

    ohr[...] = ones(one_hot(rid[0], 0, 256))
    pl.semaphore_wait(barrier, len(peers))

    send(rt, rg.at[l], gs.at[1], gr.at[1], l_other, ahead)
    send(rt, rg.at[l], gs.at[2], gr.at[2], zp, ahead)
    send(rt, rg.at[l], gs.at[3], gr.at[3], zm, ahead)
    send(rt, rg.at[l], gs.at[0], gr.at[0], l, ahead)
    send(lt, lg.at[r], ls.at[0], lr.at[0], l, yo)
    send(lt, lg.at[r], ls.at[1], lr.at[1], l, xp)
    send(lt, lg.at[r], ls.at[2], lr.at[2], l, xm)
    send(lt, lg.at[r], ls.at[3], lr.at[3], l, co)

    def ring(d, k):
        i = 2 + 4 * (d - 1) + 2 * k
        a, b = me.left_at(-d, k), me.left_at(d, k)
        n = i + 4
        arrived(rg.at[a], gr.at[i])
        up, down = (rg.at[a], rg.at[b]) if d < 3 else (rg.at[a, LOWS], rg.at[b, HIGHS])
        send(up, up, gs.at[n], gr.at[n], zp, r)
        arrived(rg.at[b], gr.at[i + 1])
        send(down, down, gs.at[n + 1], gr.at[n + 1], zm, r)

    def across(k):
        a, b = me.right_at(-1, k), me.right_at(1, k)
        ra, rb_ = (1, 2) if k == 0 else (4, 5)
        i = 7 + 4 * k
        arrived(lg.at[a], lr.at[ra])
        send(lg.at[a, LOWS], lg.at[a, LOWS], ls.at[i], lr.at[i], l, xp)
        send(lg.at[a], lg.at[a], ls.at[i + 2], lr.at[i + 2], l, co)
        arrived(lg.at[b], lr.at[rb_])
        send(lg.at[b, HIGHS], lg.at[b, HIGHS], ls.at[i + 1], lr.at[i + 1], l, xm)
        send(lg.at[b], lg.at[b], ls.at[i + 3], lr.at[i + 3], l, co)

    def far(k):
        a = me.right_at(2, k)
        i = 7 + 4 * k
        arrived(lg.at[a, LOWS], lr.at[i])
        arrived(lg.at[a, HIGHS], lr.at[i + 1])
        send(lg.at[a], lg.at[a], ls.at[15 + k], lr.at[15 + k], l, co)

    for j in range(4):
        counts(0, j)
    arrived(lg.at[yo], lr.at[0])
    send(lg.at[yo], lg.at[yo], ls.at[4], lr.at[4], l, xp)
    send(lg.at[yo], lg.at[yo], ls.at[5], lr.at[5], l, xm)
    send(lg.at[yo], lg.at[yo], ls.at[6], lr.at[6], l, co)
    across(0)
    for j in range(4, 6):
        counts(0, j)
    arrived(rg.at[l_other], gr.at[1])
    send(rg.at[l_other], rg.at[l_other], gs.at[4], gr.at[4], zp, r)
    send(rg.at[l_other], rg.at[l_other], gs.at[5], gr.at[5], zm, r)
    counts(0, 6)
    counts(0, 7)
    ring(1, 0)
    counts(1, 0)
    across(1)
    for j in range(1, 5):
        counts(1, j)
    ring(1, 1)
    for j in range(5, 8):
        counts(1, j)
    far(0)
    for j in range(3):
        source_hot(j)
    ring(2, 0)
    far(1)
    for j in range(3, 8):
        source_hot(j)
    for t in range(4):
        os_[:, TILES[t]] = dot(rel[...], ohr[:, TILES[t]])

    lcat = lambda: jnp.concatenate([lg[i] for i in range(N)], axis=1)

    def slots_of(*ds):
        zs_ = [mod(me.z + d, 8) for d in ds]
        return jnp.concatenate([rg[2 * zi + h] for zi in zs_ for h in (0, 1)], axis=1)

    def rows_from(ref, t, *ds):
        return jnp.concatenate([ref[pl.ds(rows_of(d), J), TILES[t]] for d in ds], axis=0)

    def gather_targets(*ds):
        blocks = slots_of(*ds)
        for t in range(4):
            part = dot(blocks, rows_from(oht, t, *ds))
            tt[:, TILES[t]] = part if 0 in ds else tt[:, TILES[t]] + part

    def from_negatives(*ds):
        blocks = slots_of(*ds)
        for t in range(4):
            part = dot(blocks, rows_from(w, t, *ds))
            gq[:, TILES[t]] = part if 0 in ds else gq[:, TILES[t]] + part

    def queries(t):
        s = dot(lcat(), ohs[:, TILES[t]])
        o = os_[:, TILES[t]]
        ss_[:, TILES[t]] = s
        s_re, s_im, o_re, o_im = s[:HALF], s[HALF:], o[:HALF], o[HALF:]
        q = jnp.concatenate([s_re * o_re - s_im * o_im, s_re * o_im + s_im * o_re], axis=0)
        qf[:, TILES[t]] = q
        qs[:, TILES[t]] = q.astype(BF16)

    def rows_of(d):
        return pl.multiple_of(mod(me.z + d, 8) * J, J)

    def turn(d):
        zi = mod(me.z + d, 8)
        first = rows_of(d)
        rn[pl.ds(first, B), :] = rg[2 * zi].T
        rn[pl.ds(first + B, B), :] = rg[2 * zi + 1].T

    def scores(d):
        first = rows_of(d)
        for t in range(4):
            score = dot(rn[pl.ds(first, J), :], qs[:, TILES[t]])
            m = mult[t // 2, pl.ds(first, J), :]
            m = jnp.concatenate([m, m], axis=1)
            w[pl.ds(first, J), TILES[t]] = (jax.nn.sigmoid(score) * m).astype(BF16)

    arrived(rg.at[l], gr.at[0])
    turn(0)
    gather_targets(0)
    for x, k, i in ((0, 0, 3), (0, 1, 6), (-1, 0, 9), (1, 0, 10), (-1, 1, 13), (1, 1, 14), (2, 0, 15), (2, 1, 16)):
        arrived(lg.at[me.right_at(x, k, 1)], lr.at[i])
    queries(0)
    queries(1)
    ring(2, 1)
    send(right, moved, ms.at[0], ms.at[1], l, ahead)
    send(state, moved_state, ms.at[2], ms.at[3], l, ahead)
    queries(2)
    queries(3)
    scores(0)
    from_negatives(0)
    turn(1)
    turn(-1)
    ring(3, 0)
    gather_targets(1, -1)
    scores(1)
    scores(-1)
    from_negatives(1, -1)
    ring(3, 1)
    turn(2)
    turn(-2)
    gather_targets(2, -2)
    scores(2)
    scores(-2)
    from_negatives(2, -2)
    turn(3)
    turn(-3)
    gather_targets(3, -3)
    scores(3)
    scores(-3)
    from_negatives(3, -3)
    for k in (0, 1):
        a = me.left_at(4, k)
        arrived(rg.at[a, LOWS], gr.at[14 + 2 * k])
        arrived(rg.at[a, HIGHS], gr.at[15 + 2 * k])
    turn(4)
    gather_targets(4)
    scores(4)
    from_negatives(4)

    def finish(t):
        q, target = qf[:, TILES[t]], tt[:, TILES[t]]
        positive = jnp.sum(q * target, axis=0, keepdims=True)
        pos_grad = -jax.nn.sigmoid(-positive)
        tg[:, TILES[t]] = (pos_grad * q).astype(BF16)
        g = pos_grad * target + gq[:, TILES[t]]
        sg[:, TILES[t]] = back(g, os_[:, TILES[t]]).astype(BF16)
        og[:, TILES[t]] = back(g, ss_[:, TILES[t]]).astype(BF16)

    def right_grad(d):
        zi = mod(me.z + d, 8)
        at = pl.ds(rows_of(d), J)
        part = dot_nt(qs[...], w[at, :]) + dot_nt(tg[...], oht[at, :])
        rp[2 * zi] = part[:, :B]
        rp[2 * zi + 1] = part[:, B:]

    zto, xto, sign = (zp, zm), (xp, xm), (1, -1)

    for t in range(4):
        finish(t)
    right_grad(4)
    for k in (1, 0):
        rfar[k] = rp[me.left_at(4, k)].astype(BF16)
    for k in (1, 0):
        for side in (0, 1):
            rows = pl.ds(0, LOW if side == 0 else HIGH)
            send(rfar.at[k, PART[side]], rb_half.at[side, k, rows], zs.at[side, 3, k], zr.at[side, 3, k], zto[side], r)

    def right_step(d, k):
        for side, at in ((0, me.left_at(d, k)), (1, me.left_at(-d, k))):
            mine = rp[at]
            if d == 3:
                rows = pl.ds(0, LOW if side == 0 else HIGH)
                arrived(rb_half.at[side, k, rows], zr.at[side, 3, k])
                got = rb_half[side, k, rows].astype(F32)
                if side == 0:
                    total = jnp.concatenate([mine[:LOW] + got, mine[LOW:]], axis=0)
                else:
                    total = jnp.concatenate([mine[:LOW], mine[LOW:] + got], axis=0)
            else:
                arrived(rb.at[side, d, k], zr.at[side, d, k])
                total = mine + rb[side, d, k].astype(F32)
            rstage[side, d - 1, k] = total.astype(BF16)
            send(rstage.at[side, d - 1, k], rb.at[side, d - 1, k], zs.at[side, d - 1, k], zr.at[side, d - 1, k], zto[side], r)

    part = dot_nt(ohr[...], og[...]).astype(BF16)
    for i in range(N):
        pp[i] = part[i * 16 : i * 16 + 16]
    for i in range(1, N):
        to = mod(r + i, N)
        send(pp.at[to], pbuf.at[i], ps.at[i], pr.at[i], l, to)
    right_grad(3)
    right_grad(-3)

    order = ((2, 0), (2, 1), (1, 0), (-1, 0), (1, 1), (-1, 1), (0, 0), (0, 1))

    def left_grad(n):
        x, k = order[n]
        g = lax.div(me.right_at(x, k), 2)
        part = dot_nt(sg[...], ohs[pl.ds(pl.multiple_of(g * J, J), J), :])
        lp[2 * g] = part[:, :B]
        lp[2 * g + 1] = part[:, B:]
        cst[n] = lp[me.right_at(x, k, 1)].astype(BF16)
        send(cst.at[n], cbuf.at[n], cs.at[n], cr.at[n], l, co)

    def chip_sum(n):
        x, k = order[n]
        arrived(cbuf.at[n], cr.at[n])
        return lp[me.right_at(x, k)] + cbuf[n].astype(F32)

    for n in range(4):
        left_grad(n)
    right_step(3, 1)
    right_step(3, 0)
    left_grad(4)
    left_grad(5)
    right_grad(2)
    right_grad(-2)
    total = pp[r].astype(F32)
    for i in range(1, N):
        arrived(pbuf.at[i], pr.at[i])
        total += pbuf[i].astype(F32)
    for i in range(N):
        prow[i] = total[i : i + 1]
    for i in range(1, N):
        to = mod(l + i, N)
        send(prow.at[to], qbuf.at[i], qsm.at[i], qrm.at[i], to, r)

    for k in (1, 0):
        lstage[0, k] = chip_sum(k).astype(BF16)
        for side in (0, 1):
            rows = pl.ds(0, LOW if side == 0 else HIGH)
            send(lstage.at[0, k, PART[side]], lb_half.at[side, k, rows], xs.at[side, 1, k], xr.at[side, 1, k], l, xto[side])
    left_grad(6)
    left_grad(7)
    right_grad(1)
    right_grad(-1)
    right_step(2, 1)
    right_step(2, 0)
    right_grad(0)
    for k in (1, 0):
        for side in (0, 1):
            total = chip_sum(2 + 2 * k + side)
            rows = pl.ds(0, LOW if side == 0 else HIGH)
            arrived(lb_half.at[side, k, rows], xr.at[side, 1, k])
            got = lb_half[side, k, rows].astype(F32)
            if side == 0:
                total = jnp.concatenate([total[:LOW] + got, total[LOW:]], axis=0)
            else:
                total = jnp.concatenate([total[:LOW], total[LOW:] + got], axis=0)
            lstage[1 + side, k] = total.astype(BF16)
            send(lstage.at[1 + side, k], lb.at[side, k], xs.at[side, 0, k], xr.at[side, 0, k], l, xto[side])
    total = prow[l]
    for i in range(1, N):
        arrived(qbuf.at[i], qrm.at[i])
        total += qbuf[i]
    qrow[l] = total
    for i in range(1, N):
        to = mod(l + i, N)
        send(qrow.at[l], qrow.at[l], fs.at[i], fr.at[i], to, r)

    right_step(1, 1)
    right_step(1, 0)

    for i in range(1, N):
        arrived(qrow.at[mod(l - i, N)], fr.at[i])
    total = jnp.concatenate([qrow[i] for i in range(N)], axis=0)
    fown[...] = total.astype(BF16)
    psum[r] = fown[...].astype(F32)
    for i in range(1, N):
        to = mod(r + i, N)
        send(fown, fbuf.at[i], ps.at[N + i], pr.at[N + i], l, to)

    other = rp[me.left_at(0, 1)]
    for side in (0, 1):
        arrived(rb.at[side, 0, 1], zr.at[side, 0, 1])
        other += rb[side, 0, 1].astype(F32)
    ybuf[0] = other.astype(BF16)
    send(ybuf.at[0], ybuf.at[1], ts.at[1], tr.at[1], l_other, r)
    other = chip_sum(7)
    for side in (0, 1):
        arrived(lb.at[side, 1], xr.at[side, 0, 1])
        other += lb[side, 1].astype(F32)
    lx[...] = other.astype(BF16)
    send(lx, lybuf, ts.at[0], tr.at[0], l, yo)
    total = chip_sum(6)
    for side in (0, 1):
        arrived(lb.at[side, 0], xr.at[side, 0, 0])
        total += lb[side, 0].astype(F32)
    lsum[...] = total

    total = rp[l]
    for side in (0, 1):
        arrived(rb.at[side, 0, 0], zr.at[side, 0, 0])
        total += rb[side, 0, 0].astype(F32)
    arrived(ybuf.at[1], tr.at[1])
    rsum[...] = total + ybuf[1].astype(F32)
    arrived(lybuf, tr.at[0])
    lsum[...] += lybuf[...].astype(F32)
    arrived(moved, ms.at[1])
    arrived(moved_state, ms.at[3])
    for i in range(1, N):
        arrived(fbuf.at[i], pr.at[N + i])
        psum[mod(r - i, N)] = fbuf[i].astype(F32)
    for copy in sends:
        copy.wait_send()


def bucket(left, right, state, relation, src, rid, tgt, neg):
    vm = pl.BlockSpec(memory_space=pltpu.VMEM)
    dma = pltpu.SemaphoreType.DMA
    blocks = pltpu.VMEM((N, W, B), BF16)
    return pl.pallas_call(
        bucket_kernel,
        out_shape=(
            jax.ShapeDtypeStruct((W, B), F32),
            jax.ShapeDtypeStruct((W, B), F32),
            jax.ShapeDtypeStruct((N, 16, W), F32),
            jax.ShapeDtypeStruct((W, B), F32),
            jax.ShapeDtypeStruct((1, B), F32),
        ),
        in_specs=[vm] * 8,
        out_specs=(vm,) * 5,
        scratch_shapes=[
            pltpu.VMEM((W, B), BF16),
            pltpu.VMEM((W, B), BF16),
            blocks,
            blocks,
            pltpu.VMEM((N * B, W), BF16),
            pltpu.VMEM((W, 256), BF16),
            pltpu.VMEM((N * B, E), BF16),
            pltpu.VMEM((256, E), BF16),
            pltpu.VMEM((N * B, E), BF16),
            pltpu.VMEM((W, E), BF16),
            pltpu.VMEM((W, E), F32),
            pltpu.VMEM((W, E), F32),
            pltpu.VMEM((W, E), BF16),
            pltpu.VMEM((W, E), BF16),
            pltpu.VMEM((2, N * B, B), F32),
            pltpu.VMEM((N, W, B), F32),
            pltpu.VMEM((N, W, B), F32),
            pltpu.VMEM((N, 16, W), BF16),
            pltpu.VMEM((N * B, E), BF16),
            pltpu.VMEM((W, E), F32),
            pltpu.VMEM((W, E), F32),
            pltpu.VMEM((W, E), F32),
            pltpu.VMEM((W, E), BF16),
            pltpu.VMEM((2, 2, LOW, B), BF16),
            pltpu.VMEM((2, 3, 2, W, B), BF16),
            pltpu.VMEM((2, 3, 2, W, B), BF16),
            pltpu.VMEM((2, W, B), BF16),
            pltpu.VMEM((2, W, B), BF16),
            pltpu.VMEM((8, W, B), BF16),
            pltpu.VMEM((8, W, B), BF16),
            pltpu.VMEM((2, 2, LOW, B), BF16),
            pltpu.VMEM((2, 2, W, B), BF16),
            pltpu.VMEM((3, 2, W, B), BF16),
            pltpu.VMEM((W, B), BF16),
            pltpu.VMEM((W, B), BF16),
            pltpu.VMEM((N, 16, W), BF16),
            pltpu.VMEM((N, 1, W), F32),
            pltpu.VMEM((N, 1, W), F32),
            pltpu.VMEM((N, 1, W), F32),
            pltpu.VMEM((N, 16, W), BF16),
            pltpu.VMEM((16, W), BF16),
            dma((18,)), dma((18,)), dma((17,)), dma((17,)), dma((4,)),
            dma((2, 4, 2)), dma((2, 4, 2)),
            dma((8,)), dma((8,)),
            dma((2, 2, 2)), dma((2, 2, 2)),
            dma((2 * N,)), dma((2 * N,)),
            dma((N,)), dma((N,)),
            dma((N,)), dma((N,)),
            dma((3,)), dma((2,)),
        ],
        compiler_params=pltpu.CompilerParams(collective_id=0, has_side_effects=True, vmem_limit_bytes=VMEM_LIMIT),
        name="bucket_round",
    )(left, right, state, relation, src, rid, tgt, neg)


def update_kernel(left, left_state, lsum, moved, moved_state, rsum, rel, rel_state, psum, lo, lso, ro, rso, po, pso):
    for table, state, grad, out, state_out in (
        (left, left_state, lsum[...], lo, lso),
        (moved, moved_state, rsum[...], ro, rso),
        (rel, rel_state, psum[...].reshape(256, W).T, po, pso),
    ):
        new = state[...] + jnp.sum(grad * grad, axis=0, keepdims=True) * (1.0 / W)
        state_out[...] = new
        out[...] = table[...] - LEARN_RATE * grad / jnp.sqrt(new)


def update(*args):
    vm = pl.BlockSpec(memory_space=pltpu.VMEM)
    return pl.pallas_call(
        update_kernel,
        out_shape=(
            jax.ShapeDtypeStruct((W, B), F32),
            jax.ShapeDtypeStruct((1, B), F32),
            jax.ShapeDtypeStruct((W, B), F32),
            jax.ShapeDtypeStruct((1, B), F32),
            jax.ShapeDtypeStruct((W, 256), F32),
            jax.ShapeDtypeStruct((1, 256), F32),
        ),
        in_specs=[vm] * 9,
        out_specs=(vm,) * 6,
        name="update_tables",
    )(*args)


def per_device(
    left_table,
    left_state,
    right_table,
    right_state,
    relation_table,
    relation_state,
    source_ids,
    target_ids,
    relation_ids,
    negative_ids,
):
    row = lambda state: state.reshape(1, -1)
    lsum, rsum, psum, moved, moved_state = bucket(
        left_table.T, right_table.T, row(right_state), relation_table.T, source_ids, relation_ids, target_ids, negative_ids
    )
    left_new, left_state_new, right_new, right_state_new, relation_new, relation_state_new = update(
        left_table.T, row(left_state), lsum, moved, moved_state, rsum, relation_table.T, row(relation_state), psum
    )
    flat = lambda state: state.reshape(-1)
    return (left_new.T, flat(left_state_new), right_new.T, flat(right_state_new), relation_new.T, flat(relation_state_new))


def solution(mesh):
    return jax.shard_map(
        per_device,
        mesh=mesh,
        in_specs=(
            P(("left", "right"), None),
            P(("left", "right")),
            P(("left", "right"), None),
            P(("left", "right")),
            P(),
            P(),
            P("left", "right", None),
            P("left", "right", None),
            P("left", "right", None),
            P("left", "right", None, None),
        ),
        out_specs=(
            P(("left", "right"), None),
            P(("left", "right")),
            P(("left", "right"), None),
            P(("left", "right")),
            P(),
            P(),
        ),
        check_vma=False,
    )
```

```python
import functools

import jax
import jax.numpy as jnp
from jax import lax
from jax.experimental import pallas as pl
from jax.experimental.pallas import tpu as pltpu
from jax.sharding import PartitionSpec as P

LEARN_RATE = 0.1
NEG_WEIGHT = 0.03125
MESH = pl.DeviceIdType.MESH
F32, BF16 = jnp.float32, jnp.bfloat16

N = 16
W = 400
HALF = 200
B = 128
LOW = 208
HIGH = W - LOW
VMEM_LIMIT = 60 * 1024 * 1024


def mod(value, n):
    return lax.rem(value + 4 * n, n)


class Place:
    def __init__(self):
        self.l = lax.axis_index("left")
        self.r = lax.axis_index("right")
        self.z = lax.div(self.l, 2)
        self.h = lax.rem(self.l, 2)
        self.c = lax.rem(self.r, 2)
        self.x = lax.rem(lax.div(self.r, 2), 4)
        self.yl = lax.div(self.r, 8)

    def left_at(self, z, k=0):
        h = self.h if k == 0 else 1 - self.h
        return mod(self.z + z, 8) * 2 + h

    def right_at(self, x, k=0, other=0):
        yl = self.yl if k == 0 else 1 - self.yl
        c = self.c if other == 0 else 1 - self.c
        return (yl * 4 + mod(self.x + x, 4)) * 2 + c


def remote(src, dst, send, recv, left, right):
    return pltpu.make_async_remote_copy(
        src_ref=src,
        dst_ref=dst,
        send_sem=send,
        recv_sem=recv,
        device_id=(left, right),
        device_id_type=MESH,
    )


E = 1024
T = 256
TILES = tuple(slice(t * T, t * T + T) for t in range(E // T))
J = 256
LOWS, HIGHS = pl.ds(0, LOW), pl.ds(LOW, HIGH)
PART = (LOWS, HIGHS)


def one_hot(ids, first, rows):
    row = lax.broadcasted_iota(jnp.int32, (rows, ids.shape[-1]), 0)
    return row == ids - first


def ones(hit):
    return jnp.where(hit, 1.0, 0.0).astype(BF16)


def back(g, o):
    g_re, g_im, o_re, o_im = g[:HALF], g[HALF:], o[:HALF], o[HALF:]
    return jnp.concatenate([g_re * o_re + g_im * o_im, g_im * o_re - g_re * o_im], axis=0)


def dot(a, b):
    return lax.dot_general(a, b, (((1,), (0,)), ((), ())), preferred_element_type=F32)


def dot_nt(a, b):
    return lax.dot_general(a, b, (((1,), (1,)), ((), ())), preferred_element_type=F32)


def bucket_kernel(
    left, right, state, relation, src, rid, tgt, neg,
    lsum, rsum, psum, moved, moved_state,
    lt, rt, lg, rg, rn, rel, ohs, ohr, w, qs, ss_, os_, sg, og, mult,
    rp, lp, pp, oht, tt, gq, qf, tg,
    rb_half, rb, rstage, rfar, ybuf, cst, cbuf, lb_half, lb, lstage, lx, lybuf,
    pbuf, prow, qbuf, qrow, fbuf, fown,
    gs, gr, ls, lr, ms,
    zs, zr, cs, cr, xs, xr, ps, pr, qsm, qrm, fs, fr, ts, tr,
):
    me = Place()
    l, r = me.l, me.r
    ahead, behind = mod(r + 1, N), mod(r - 1, N)
    l_other = me.left_at(0, 1)
    zp, zm = me.left_at(1), me.left_at(-1)
    xp, xm = me.right_at(1), me.right_at(-1)
    yo, co = me.right_at(0, 1), me.right_at(0, 0, 1)
    barrier = pltpu.get_barrier_semaphore()

    def greet(a, b):
        pl.semaphore_signal(barrier, inc=1, device_id=(a, b), device_id_type=MESH)

    peers = [(l_other, ahead), (l_other, behind)]
    peers += [(l, mod(r + i, N)) for i in range(1, N)] + [(mod(l + i, N), r) for i in range(1, N)]
    for a, b in peers:
        greet(a, b)

    sends = []

    def send(src_ref, dst, s, d, a, b):
        copy = remote(src_ref, dst, s, d, a, b)
        copy.start()
        sends.append(copy)

    def arrived(dst, d):
        remote(dst, dst, ts.at[2], d, l, co).wait_recv()

    rt[...] = right[...].astype(BF16)
    lt[...] = left[...].astype(BF16)
    lg[r] = lt[...]
    rel[...] = relation[...].astype(BF16)
    ids = lambda ref, t: ref[0, :, TILES[t]]

    def counts(c):
        named = neg[0, 0, c : c + 1, :]
        low_hot = ones(one_hot(lax.bitwise_and(named, B - 1), 0, B))
        block_hot = ones(one_hot(lax.shift_right_logical(named, 7), 0, B))
        count = dot_nt(low_hot, block_hot) * NEG_WEIGHT
        for i in range(N):
            mult[c, pl.ds(i * B, B), :] = jnp.broadcast_to(count[:, i : i + 1], (B, B))

    def source_hot(j):
        ohs[pl.ds(j * J, J), :] = ones(one_hot(src[0], j * J, J))
        oht[pl.ds(j * J, J), :] = ones(one_hot(tgt[0], j * J, J))

    ohr[...] = ones(one_hot(rid[0], 0, 256))
    pl.semaphore_wait(barrier, len(peers))

    send(rt, rg.at[l], gs.at[0], gr.at[0], l, ahead)
    send(rt, rg.at[l], gs.at[1], gr.at[1], l_other, ahead)
    send(lt, lg.at[r], ls.at[0], lr.at[0], l, yo)
    send(lt, lg.at[r], ls.at[1], lr.at[1], l, xp)
    send(lt, lg.at[r], ls.at[2], lr.at[2], l, xm)
    send(lt, lg.at[r], ls.at[3], lr.at[3], l, co)

    def ring(d, k):
        i = 2 + 4 * (d - 1) + 2 * k
        a, b = me.left_at(-d, k), me.left_at(d, k)
        n = i + 4
        arrived(rg.at[a], gr.at[i])
        up, down = (rg.at[a], rg.at[b]) if d < 3 else (rg.at[a, LOWS], rg.at[b, HIGHS])
        send(up, up, gs.at[n], gr.at[n], zp, r)
        arrived(rg.at[b], gr.at[i + 1])
        send(down, down, gs.at[n + 1], gr.at[n + 1], zm, r)

    def across(k):
        a, b = me.right_at(-1, k), me.right_at(1, k)
        ra, rb_ = (1, 2) if k == 0 else (4, 5)
        i = 7 + 4 * k
        arrived(lg.at[a], lr.at[ra])
        send(lg.at[a, LOWS], lg.at[a, LOWS], ls.at[i], lr.at[i], l, xp)
        send(lg.at[a], lg.at[a], ls.at[i + 2], lr.at[i + 2], l, co)
        arrived(lg.at[b], lr.at[rb_])
        send(lg.at[b, HIGHS], lg.at[b, HIGHS], ls.at[i + 1], lr.at[i + 1], l, xm)
        send(lg.at[b], lg.at[b], ls.at[i + 3], lr.at[i + 3], l, co)

    def far(k):
        a = me.right_at(2, k)
        i = 7 + 4 * k
        arrived(lg.at[a, LOWS], lr.at[i])
        arrived(lg.at[a, HIGHS], lr.at[i + 1])
        send(lg.at[a], lg.at[a], ls.at[15 + k], lr.at[15 + k], l, co)

    lcat = lambda: jnp.concatenate([lg[i] for i in range(N)], axis=1)

    def slots_of(*ds):
        zs_ = [mod(me.z + d, 8) for d in ds]
        return jnp.concatenate([rg[2 * zi + h] for zi in zs_ for h in (0, 1)], axis=1)

    def rows_from(ref, t, *ds):
        return jnp.concatenate([ref[pl.ds(rows_of(d), J), TILES[t]] for d in ds], axis=0)

    def gather_targets(*ds):
        blocks = slots_of(*ds)
        for t in range(4):
            part = dot(blocks, rows_from(oht, t, *ds))
            tt[:, TILES[t]] = part if 0 in ds else tt[:, TILES[t]] + part

    def from_negatives(*ds):
        blocks = slots_of(*ds)
        for t in range(4):
            part = dot(blocks, rows_from(w, t, *ds))
            gq[:, TILES[t]] = part if 0 in ds else gq[:, TILES[t]] + part

    def queries(t):
        s = dot(lcat(), ohs[:, TILES[t]])
        o = os_[:, TILES[t]]
        ss_[:, TILES[t]] = s
        s_re, s_im, o_re, o_im = s[:HALF], s[HALF:], o[:HALF], o[HALF:]
        q = jnp.concatenate([s_re * o_re - s_im * o_im, s_re * o_im + s_im * o_re], axis=0)
        qf[:, TILES[t]] = q
        qs[:, TILES[t]] = q.astype(BF16)

    def rows_of(d):
        return pl.multiple_of(mod(me.z + d, 8) * J, J)

    def turn(d):
        zi = mod(me.z + d, 8)
        first = rows_of(d)
        rn[pl.ds(first, B), :] = rg[2 * zi].T
        rn[pl.ds(first + B, B), :] = rg[2 * zi + 1].T

    def scores(d):
        first = rows_of(d)
        for t in range(4):
            score = dot(rn[pl.ds(first, J), :], qs[:, TILES[t]])
            m = mult[t // 2, pl.ds(first, J), :]
            m = jnp.concatenate([m, m], axis=1)
            w[pl.ds(first, J), TILES[t]] = (jax.nn.sigmoid(score) * m).astype(BF16)

    counts(0)
    counts(1)
    arrived(rg.at[l], gr.at[0])
    send(rg.at[l], rg.at[l], gs.at[2], gr.at[2], zp, r)
    send(rg.at[l], rg.at[l], gs.at[3], gr.at[3], zm, r)
    arrived(lg.at[yo], lr.at[0])
    send(lg.at[yo], lg.at[yo], ls.at[4], lr.at[4], l, xp)
    send(lg.at[yo], lg.at[yo], ls.at[5], lr.at[5], l, xm)
    send(lg.at[yo], lg.at[yo], ls.at[6], lr.at[6], l, co)
    across(0)
    source_hot(0)
    source_hot(1)
    arrived(rg.at[l_other], gr.at[1])
    send(rg.at[l_other], rg.at[l_other], gs.at[4], gr.at[4], zp, r)
    send(rg.at[l_other], rg.at[l_other], gs.at[5], gr.at[5], zm, r)
    for j in range(2, 6):
        source_hot(j)
    ring(1, 0)
    across(1)
    source_hot(6)
    source_hot(7)
    turn(0)
    gather_targets(0)
    far(0)
    ring(1, 1)
    for t in range(4):
        os_[:, TILES[t]] = dot(rel[...], ohr[:, TILES[t]])
    far(1)
    turn(1)
    turn(-1)
    ring(2, 0)
    gather_targets(1, -1)
    for x, k, i in ((0, 0, 3), (0, 1, 6), (-1, 0, 9), (1, 0, 10), (-1, 1, 13), (1, 1, 14), (2, 0, 15), (2, 1, 16)):
        arrived(lg.at[me.right_at(x, k, 1)], lr.at[i])
    queries(0)
    queries(1)
    ring(2, 1)
    send(right, moved, ms.at[0], ms.at[1], l, ahead)
    send(state, moved_state, ms.at[2], ms.at[3], l, ahead)
    queries(2)
    queries(3)
    scores(0)
    from_negatives(0)
    scores(1)
    ring(3, 0)
    scores(-1)
    from_negatives(1, -1)
    turn(2)
    turn(-2)
    gather_targets(2, -2)
    scores(2)
    ring(3, 1)
    scores(-2)
    from_negatives(2, -2)
    turn(3)
    turn(-3)
    gather_targets(3, -3)
    scores(3)
    scores(-3)
    from_negatives(3, -3)
    for k in (0, 1):
        a = me.left_at(4, k)
        arrived(rg.at[a, LOWS], gr.at[14 + 2 * k])
        arrived(rg.at[a, HIGHS], gr.at[15 + 2 * k])
    turn(4)
    gather_targets(4)
    scores(4)
    from_negatives(4)

    def finish(t):
        q, target = qf[:, TILES[t]], tt[:, TILES[t]]
        positive = jnp.sum(q * target, axis=0, keepdims=True)
        pos_grad = -jax.nn.sigmoid(-positive)
        tg[:, TILES[t]] = (pos_grad * q).astype(BF16)
        g = pos_grad * target + gq[:, TILES[t]]
        sg[:, TILES[t]] = back(g, os_[:, TILES[t]]).astype(BF16)
        og[:, TILES[t]] = back(g, ss_[:, TILES[t]]).astype(BF16)

    def right_grad(d):
        zi = mod(me.z + d, 8)
        at = pl.ds(rows_of(d), J)
        part = dot_nt(qs[...], w[at, :]) + dot_nt(tg[...], oht[at, :])
        rp[2 * zi] = part[:, :B]
        rp[2 * zi + 1] = part[:, B:]

    zto, xto, sign = (zp, zm), (xp, xm), (1, -1)

    for t in range(4):
        finish(t)
    right_grad(4)
    for k in (1, 0):
        rfar[k] = rp[me.left_at(4, k)].astype(BF16)
    for k in (1, 0):
        for side in (0, 1):
            rows = pl.ds(0, LOW if side == 0 else HIGH)
            send(rfar.at[k, PART[side]], rb_half.at[side, k, rows], zs.at[side, 3, k], zr.at[side, 3, k], zto[side], r)

    def right_step(d, k):
        for side, at in ((0, me.left_at(d, k)), (1, me.left_at(-d, k))):
            mine = rp[at]
            if d == 3:
                rows = pl.ds(0, LOW if side == 0 else HIGH)
                arrived(rb_half.at[side, k, rows], zr.at[side, 3, k])
                got = rb_half[side, k, rows].astype(F32)
                if side == 0:
                    total = jnp.concatenate([mine[:LOW] + got, mine[LOW:]], axis=0)
                else:
                    total = jnp.concatenate([mine[:LOW], mine[LOW:] + got], axis=0)
            else:
                arrived(rb.at[side, d, k], zr.at[side, d, k])
                total = mine + rb[side, d, k].astype(F32)
            rstage[side, d - 1, k] = total.astype(BF16)
            send(rstage.at[side, d - 1, k], rb.at[side, d - 1, k], zs.at[side, d - 1, k], zr.at[side, d - 1, k], zto[side], r)

    part = dot_nt(ohr[...], og[...]).astype(BF16)
    for i in range(N):
        pp[i] = part[i * 16 : i * 16 + 16]
    for i in range(1, N):
        to = mod(r + i, N)
        send(pp.at[to], pbuf.at[i], ps.at[i], pr.at[i], l, to)
    right_grad(3)
    right_grad(-3)

    order = ((2, 0), (2, 1), (1, 0), (-1, 0), (1, 1), (-1, 1), (0, 0), (0, 1))

    def left_grad(n):
        x, k = order[n]
        g = lax.div(me.right_at(x, k), 2)
        part = dot_nt(sg[...], ohs[pl.ds(pl.multiple_of(g * J, J), J), :])
        lp[2 * g] = part[:, :B]
        lp[2 * g + 1] = part[:, B:]
        cst[n] = lp[me.right_at(x, k, 1)].astype(BF16)
        send(cst.at[n], cbuf.at[n], cs.at[n], cr.at[n], l, co)

    def chip_sum(n):
        x, k = order[n]
        arrived(cbuf.at[n], cr.at[n])
        return lp[me.right_at(x, k)] + cbuf[n].astype(F32)

    for n in range(4):
        left_grad(n)
    right_step(3, 1)
    right_step(3, 0)
    left_grad(4)
    left_grad(5)
    right_grad(2)
    right_grad(-2)
    total = pp[r].astype(F32)
    for i in range(1, N):
        arrived(pbuf.at[i], pr.at[i])
        total += pbuf[i].astype(F32)
    for i in range(N):
        prow[i] = total[i : i + 1]
    for i in range(1, N):
        to = mod(l + i, N)
        send(prow.at[to], qbuf.at[i], qsm.at[i], qrm.at[i], to, r)

    for k in (1, 0):
        lstage[0, k] = chip_sum(k).astype(BF16)
        for side in (0, 1):
            rows = pl.ds(0, LOW if side == 0 else HIGH)
            send(lstage.at[0, k, PART[side]], lb_half.at[side, k, rows], xs.at[side, 1, k], xr.at[side, 1, k], l, xto[side])
    left_grad(6)
    left_grad(7)
    right_grad(1)
    right_grad(-1)
    right_step(2, 1)
    right_step(2, 0)
    right_grad(0)
    for k in (1, 0):
        for side in (0, 1):
            total = chip_sum(2 + 2 * k + side)
            rows = pl.ds(0, LOW if side == 0 else HIGH)
            arrived(lb_half.at[side, k, rows], xr.at[side, 1, k])
            got = lb_half[side, k, rows].astype(F32)
            if side == 0:
                total = jnp.concatenate([total[:LOW] + got, total[LOW:]], axis=0)
            else:
                total = jnp.concatenate([total[:LOW], total[LOW:] + got], axis=0)
            lstage[1 + side, k] = total.astype(BF16)
            send(lstage.at[1 + side, k], lb.at[side, k], xs.at[side, 0, k], xr.at[side, 0, k], l, xto[side])
    total = prow[l]
    for i in range(1, N):
        arrived(qbuf.at[i], qrm.at[i])
        total += qbuf[i]
    qrow[l] = total
    for i in range(1, N):
        to = mod(l + i, N)
        send(qrow.at[l], qrow.at[l], fs.at[i], fr.at[i], to, r)

    right_step(1, 1)
    right_step(1, 0)

    for i in range(1, N):
        arrived(qrow.at[mod(l - i, N)], fr.at[i])
    total = jnp.concatenate([qrow[i] for i in range(N)], axis=0)
    fown[...] = total.astype(BF16)
    psum[r] = fown[...].astype(F32)
    for i in range(1, N):
        to = mod(r + i, N)
        send(fown, fbuf.at[i], ps.at[N + i], pr.at[N + i], l, to)

    other = rp[me.left_at(0, 1)]
    for side in (0, 1):
        arrived(rb.at[side, 0, 1], zr.at[side, 0, 1])
        other += rb[side, 0, 1].astype(F32)
    ybuf[0] = other.astype(BF16)
    send(ybuf.at[0], ybuf.at[1], ts.at[1], tr.at[1], l_other, r)
    other = chip_sum(7)
    for side in (0, 1):
        arrived(lb.at[side, 1], xr.at[side, 0, 1])
        other += lb[side, 1].astype(F32)
    lx[...] = other.astype(BF16)
    send(lx, lybuf, ts.at[0], tr.at[0], l, yo)
    total = chip_sum(6)
    for side in (0, 1):
        arrived(lb.at[side, 0], xr.at[side, 0, 0])
        total += lb[side, 0].astype(F32)
    lsum[...] = total

    total = rp[l]
    for side in (0, 1):
        arrived(rb.at[side, 0, 0], zr.at[side, 0, 0])
        total += rb[side, 0, 0].astype(F32)
    arrived(ybuf.at[1], tr.at[1])
    rsum[...] = total + ybuf[1].astype(F32)
    arrived(lybuf, tr.at[0])
    lsum[...] += lybuf[...].astype(F32)
    arrived(moved, ms.at[1])
    arrived(moved_state, ms.at[3])
    for i in range(1, N):
        arrived(fbuf.at[i], pr.at[N + i])
        psum[mod(r - i, N)] = fbuf[i].astype(F32)
    for copy in sends:
        copy.wait_send()


def bucket(left, right, state, relation, src, rid, tgt, neg):
    vm = pl.BlockSpec(memory_space=pltpu.VMEM)
    dma = pltpu.SemaphoreType.DMA
    blocks = pltpu.VMEM((N, W, B), BF16)
    return pl.pallas_call(
        bucket_kernel,
        out_shape=(
            jax.ShapeDtypeStruct((W, B), F32),
            jax.ShapeDtypeStruct((W, B), F32),
            jax.ShapeDtypeStruct((N, 16, W), F32),
            jax.ShapeDtypeStruct((W, B), F32),
            jax.ShapeDtypeStruct((1, B), F32),
        ),
        in_specs=[vm] * 8,
        out_specs=(vm,) * 5,
        scratch_shapes=[
            pltpu.VMEM((W, B), BF16),
            pltpu.VMEM((W, B), BF16),
            blocks,
            blocks,
            pltpu.VMEM((N * B, W), BF16),
            pltpu.VMEM((W, 256), BF16),
            pltpu.VMEM((N * B, E), BF16),
            pltpu.VMEM((256, E), BF16),
            pltpu.VMEM((N * B, E), BF16),
            pltpu.VMEM((W, E), BF16),
            pltpu.VMEM((W, E), F32),
            pltpu.VMEM((W, E), F32),
            pltpu.VMEM((W, E), BF16),
            pltpu.VMEM((W, E), BF16),
            pltpu.VMEM((2, N * B, B), F32),
            pltpu.VMEM((N, W, B), F32),
            pltpu.VMEM((N, W, B), F32),
            pltpu.VMEM((N, 16, W), BF16),
            pltpu.VMEM((N * B, E), BF16),
            pltpu.VMEM((W, E), F32),
            pltpu.VMEM((W, E), F32),
            pltpu.VMEM((W, E), F32),
            pltpu.VMEM((W, E), BF16),
            pltpu.VMEM((2, 2, LOW, B), BF16),
            pltpu.VMEM((2, 3, 2, W, B), BF16),
            pltpu.VMEM((2, 3, 2, W, B), BF16),
            pltpu.VMEM((2, W, B), BF16),
            pltpu.VMEM((2, W, B), BF16),
            pltpu.VMEM((8, W, B), BF16),
            pltpu.VMEM((8, W, B), BF16),
            pltpu.VMEM((2, 2, LOW, B), BF16),
            pltpu.VMEM((2, 2, W, B), BF16),
            pltpu.VMEM((3, 2, W, B), BF16),
            pltpu.VMEM((W, B), BF16),
            pltpu.VMEM((W, B), BF16),
            pltpu.VMEM((N, 16, W), BF16),
            pltpu.VMEM((N, 1, W), F32),
            pltpu.VMEM((N, 1, W), F32),
            pltpu.VMEM((N, 1, W), F32),
            pltpu.VMEM((N, 16, W), BF16),
            pltpu.VMEM((16, W), BF16),
            dma((18,)), dma((18,)), dma((17,)), dma((17,)), dma((4,)),
            dma((2, 4, 2)), dma((2, 4, 2)),
            dma((8,)), dma((8,)),
            dma((2, 2, 2)), dma((2, 2, 2)),
            dma((2 * N,)), dma((2 * N,)),
            dma((N,)), dma((N,)),
            dma((N,)), dma((N,)),
            dma((3,)), dma((2,)),
        ],
        compiler_params=pltpu.CompilerParams(collective_id=0, has_side_effects=True, vmem_limit_bytes=VMEM_LIMIT),
        name="bucket_round",
    )(left, right, state, relation, src, rid, tgt, neg)


def update_kernel(left, left_state, lsum, moved, moved_state, rsum, rel, rel_state, psum, lo, lso, ro, rso, po, pso):
    for table, state, grad, out, state_out in (
        (left, left_state, lsum[...], lo, lso),
        (moved, moved_state, rsum[...], ro, rso),
        (rel, rel_state, psum[...].reshape(256, W).T, po, pso),
    ):
        new = state[...] + jnp.sum(grad * grad, axis=0, keepdims=True) * (1.0 / W)
        state_out[...] = new
        out[...] = table[...] - LEARN_RATE * grad / jnp.sqrt(new)


def update(*args):
    vm = pl.BlockSpec(memory_space=pltpu.VMEM)
    return pl.pallas_call(
        update_kernel,
        out_shape=(
            jax.ShapeDtypeStruct((W, B), F32),
            jax.ShapeDtypeStruct((1, B), F32),
            jax.ShapeDtypeStruct((W, B), F32),
            jax.ShapeDtypeStruct((1, B), F32),
            jax.ShapeDtypeStruct((W, 256), F32),
            jax.ShapeDtypeStruct((1, 256), F32),
        ),
        in_specs=[vm] * 9,
        out_specs=(vm,) * 6,
        name="update_tables",
    )(*args)


def per_device(
    left_table,
    left_state,
    right_table,
    right_state,
    relation_table,
    relation_state,
    source_ids,
    target_ids,
    relation_ids,
    negative_ids,
):
    row = lambda state: state.reshape(1, -1)
    lsum, rsum, psum, moved, moved_state = bucket(
        left_table.T, right_table.T, row(right_state), relation_table.T, source_ids, relation_ids, target_ids, negative_ids
    )
    left_new, left_state_new, right_new, right_state_new, relation_new, relation_state_new = update(
        left_table.T, row(left_state), lsum, moved, moved_state, rsum, relation_table.T, row(relation_state), psum
    )
    flat = lambda state: state.reshape(-1)
    return (left_new.T, flat(left_state_new), right_new.T, flat(right_state_new), relation_new.T, flat(relation_state_new))


def solution(mesh):
    return jax.shard_map(
        per_device,
        mesh=mesh,
        in_specs=(
            P(("left", "right"), None),
            P(("left", "right")),
            P(("left", "right"), None),
            P(("left", "right")),
            P(),
            P(),
            P("left", "right", None),
            P("left", "right", None),
            P("left", "right", None),
            P("left", "right", None, None),
        ),
        out_specs=(
            P(("left", "right"), None),
            P(("left", "right")),
            P(("left", "right"), None),
            P(("left", "right")),
            P(),
            P(),
        ),
        check_vma=False,
    )
```

```python
import functools

import jax
import jax.numpy as jnp
from jax import lax
from jax.experimental import pallas as pl
from jax.experimental.pallas import tpu as pltpu
from jax.sharding import PartitionSpec as P

LEARN_RATE = 0.1
NEG_WEIGHT = 0.03125
MESH = pl.DeviceIdType.MESH
F32, BF16 = jnp.float32, jnp.bfloat16

N = 16
W = 400
HALF = 200
B = 128
LOW = 208
HIGH = W - LOW
VMEM_LIMIT = 60 * 1024 * 1024


def mod(value, n):
    return lax.rem(value + 4 * n, n)


class Place:
    def __init__(self):
        self.l = lax.axis_index("left")
        self.r = lax.axis_index("right")
        self.z = lax.div(self.l, 2)
        self.h = lax.rem(self.l, 2)
        self.c = lax.rem(self.r, 2)
        self.x = lax.rem(lax.div(self.r, 2), 4)
        self.yl = lax.div(self.r, 8)

    def left_at(self, z, k=0):
        h = self.h if k == 0 else 1 - self.h
        return mod(self.z + z, 8) * 2 + h

    def right_at(self, x, k=0, other=0):
        yl = self.yl if k == 0 else 1 - self.yl
        c = self.c if other == 0 else 1 - self.c
        return (yl * 4 + mod(self.x + x, 4)) * 2 + c


def remote(src, dst, send, recv, left, right):
    return pltpu.make_async_remote_copy(
        src_ref=src,
        dst_ref=dst,
        send_sem=send,
        recv_sem=recv,
        device_id=(left, right),
        device_id_type=MESH,
    )


E = 1024
T = 256
TILES = tuple(slice(t * T, t * T + T) for t in range(E // T))
J = 256
LOWS, HIGHS = pl.ds(0, LOW), pl.ds(LOW, HIGH)
PART = (LOWS, HIGHS)


def one_hot(ids, first, rows):
    row = lax.broadcasted_iota(jnp.int32, (rows, ids.shape[-1]), 0)
    return row == ids - first


def ones(hit):
    return jnp.where(hit, 1.0, 0.0).astype(BF16)


def back(g, o):
    g_re, g_im, o_re, o_im = g[:HALF], g[HALF:], o[:HALF], o[HALF:]
    return jnp.concatenate([g_re * o_re + g_im * o_im, g_im * o_re - g_re * o_im], axis=0)


def dot(a, b):
    return lax.dot_general(a, b, (((1,), (0,)), ((), ())), preferred_element_type=F32)


def dot_nt(a, b):
    return lax.dot_general(a, b, (((1,), (1,)), ((), ())), preferred_element_type=F32)


def bucket_kernel(
    left, right, state, relation, src, rid, tgt, neg,
    lsum, rsum, psum, moved, moved_state,
    lt, rt, lg, rg, rn, rel, ohs, ohr, w, qs, ss_, os_, sg, og, mult,
    rp, lp, pp, oht, tt, gq, qf, tg,
    rb_half, rb, rstage, rfar, ybuf, cst, cbuf, lb_half, lb, lstage, lx, lybuf,
    pbuf, prow, qbuf, qrow, fbuf, fown,
    gs, gr, ls, lr, ms,
    zs, zr, cs, cr, xs, xr, ps, pr, qsm, qrm, fs, fr, ts, tr,
):
    me = Place()
    l, r = me.l, me.r
    ahead, behind = mod(r + 1, N), mod(r - 1, N)
    l_other = me.left_at(0, 1)
    zp, zm = me.left_at(1), me.left_at(-1)
    xp, xm = me.right_at(1), me.right_at(-1)
    yo, co = me.right_at(0, 1), me.right_at(0, 0, 1)
    barrier = pltpu.get_barrier_semaphore()

    def greet(a, b):
        pl.semaphore_signal(barrier, inc=1, device_id=(a, b), device_id_type=MESH)

    peers = [(l_other, ahead), (l_other, behind)]
    peers += [(l, mod(r + i, N)) for i in range(1, N)] + [(mod(l + i, N), r) for i in range(1, N)]
    for a, b in peers:
        greet(a, b)

    sends = []

    def send(src_ref, dst, s, d, a, b):
        copy = remote(src_ref, dst, s, d, a, b)
        copy.start()
        sends.append(copy)

    def arrived(dst, d):
        remote(dst, dst, ts.at[2], d, l, co).wait_recv()

    rt[...] = right[...].astype(BF16)
    lt[...] = left[...].astype(BF16)
    lg[r] = lt[...]
    rel[...] = relation[...].astype(BF16)
    ids = lambda ref, t: ref[0, :, TILES[t]]

    def counts(c):
        named = neg[0, 0, c : c + 1, :]
        low_hot = ones(one_hot(lax.bitwise_and(named, B - 1), 0, B))
        block_hot = ones(one_hot(lax.shift_right_logical(named, 7), 0, B))
        count = dot_nt(low_hot, block_hot) * NEG_WEIGHT
        for i in range(N):
            mult[c, pl.ds(i * B, B), :] = jnp.broadcast_to(count[:, i : i + 1], (B, B))

    def source_hot(j):
        ohs[pl.ds(j * J, J), :] = ones(one_hot(src[0], j * J, J))
        oht[pl.ds(j * J, J), :] = ones(one_hot(tgt[0], j * J, J))

    ohr[...] = ones(one_hot(rid[0], 0, 256))
    pl.semaphore_wait(barrier, len(peers))

    send(rt, rg.at[l], gs.at[0], gr.at[0], l, ahead)
    send(rt, rg.at[l], gs.at[1], gr.at[1], l_other, ahead)
    send(lt, lg.at[r], ls.at[0], lr.at[0], l, yo)
    send(lt, lg.at[r], ls.at[1], lr.at[1], l, xp)
    send(lt, lg.at[r], ls.at[2], lr.at[2], l, xm)
    send(lt, lg.at[r], ls.at[3], lr.at[3], l, co)

    def ring(d, k):
        i = 2 + 4 * (d - 1) + 2 * k
        a, b = me.left_at(-d, k), me.left_at(d, k)
        n = i + 4
        arrived(rg.at[a], gr.at[i])
        up, down = (rg.at[a], rg.at[b]) if d < 3 else (rg.at[a, LOWS], rg.at[b, HIGHS])
        send(up, up, gs.at[n], gr.at[n], zp, r)
        arrived(rg.at[b], gr.at[i + 1])
        send(down, down, gs.at[n + 1], gr.at[n + 1], zm, r)

    def across(k):
        a, b = me.right_at(-1, k), me.right_at(1, k)
        ra, rb_ = (1, 2) if k == 0 else (4, 5)
        i = 7 + 4 * k
        arrived(lg.at[a], lr.at[ra])
        send(lg.at[a, LOWS], lg.at[a, LOWS], ls.at[i], lr.at[i], l, xp)
        send(lg.at[a], lg.at[a], ls.at[i + 2], lr.at[i + 2], l, co)
        arrived(lg.at[b], lr.at[rb_])
        send(lg.at[b, HIGHS], lg.at[b, HIGHS], ls.at[i + 1], lr.at[i + 1], l, xm)
        send(lg.at[b], lg.at[b], ls.at[i + 3], lr.at[i + 3], l, co)

    def far(k):
        a = me.right_at(2, k)
        i = 7 + 4 * k
        arrived(lg.at[a, LOWS], lr.at[i])
        arrived(lg.at[a, HIGHS], lr.at[i + 1])
        send(lg.at[a], lg.at[a], ls.at[15 + k], lr.at[15 + k], l, co)

    lcat = lambda: jnp.concatenate([lg[i] for i in range(N)], axis=1)

    def slots_of(*ds):
        zs_ = [mod(me.z + d, 8) for d in ds]
        return jnp.concatenate([rg[2 * zi + h] for zi in zs_ for h in (0, 1)], axis=1)

    def rows_from(ref, t, *ds):
        return jnp.concatenate([ref[pl.ds(rows_of(d), J), TILES[t]] for d in ds], axis=0)

    def gather_targets(*ds):
        blocks = slots_of(*ds)
        for t in range(4):
            part = dot(blocks, rows_from(oht, t, *ds))
            tt[:, TILES[t]] = part if 0 in ds else tt[:, TILES[t]] + part

    def from_negatives(*ds):
        blocks = slots_of(*ds)
        for t in range(4):
            part = dot(blocks, rows_from(w, t, *ds))
            gq[:, TILES[t]] = part if 0 in ds else gq[:, TILES[t]] + part

    def queries(t):
        s = dot(lcat(), ohs[:, TILES[t]])
        o = os_[:, TILES[t]]
        ss_[:, TILES[t]] = s
        s_re, s_im, o_re, o_im = s[:HALF], s[HALF:], o[:HALF], o[HALF:]
        q = jnp.concatenate([s_re * o_re - s_im * o_im, s_re * o_im + s_im * o_re], axis=0)
        qf[:, TILES[t]] = q
        qs[:, TILES[t]] = q.astype(BF16)

    def rows_of(d):
        return pl.multiple_of(mod(me.z + d, 8) * J, J)

    def turn(d):
        zi = mod(me.z + d, 8)
        first = rows_of(d)
        rn[pl.ds(first, B), :] = rg[2 * zi].T
        rn[pl.ds(first + B, B), :] = rg[2 * zi + 1].T

    def scores(d):
        first = rows_of(d)
        for t in range(4):
            score = dot(rn[pl.ds(first, J), :], qs[:, TILES[t]])
            m = mult[t // 2, pl.ds(first, J), :]
            m = jnp.concatenate([m, m], axis=1)
            w[pl.ds(first, J), TILES[t]] = (jax.nn.sigmoid(score) * m).astype(BF16)

    counts(0)
    counts(1)
    arrived(rg.at[l], gr.at[0])
    send(rg.at[l], rg.at[l], gs.at[2], gr.at[2], zp, r)
    send(rg.at[l], rg.at[l], gs.at[3], gr.at[3], zm, r)
    arrived(lg.at[yo], lr.at[0])
    send(lg.at[yo], lg.at[yo], ls.at[4], lr.at[4], l, xp)
    send(lg.at[yo], lg.at[yo], ls.at[5], lr.at[5], l, xm)
    send(lg.at[yo], lg.at[yo], ls.at[6], lr.at[6], l, co)
    across(0)
    source_hot(0)
    source_hot(1)
    arrived(rg.at[l_other], gr.at[1])
    send(rg.at[l_other], rg.at[l_other], gs.at[4], gr.at[4], zp, r)
    send(rg.at[l_other], rg.at[l_other], gs.at[5], gr.at[5], zm, r)
    for j in range(2, 6):
        source_hot(j)
    ring(1, 0)
    across(1)
    source_hot(6)
    source_hot(7)
    turn(0)
    gather_targets(0)
    far(0)
    ring(1, 1)
    for t in range(4):
        os_[:, TILES[t]] = dot(rel[...], ohr[:, TILES[t]])
    far(1)
    turn(1)
    turn(-1)
    ring(2, 0)
    gather_targets(1, -1)
    for x, k, i in ((0, 0, 3), (0, 1, 6), (-1, 0, 9), (1, 0, 10), (-1, 1, 13), (1, 1, 14), (2, 0, 15), (2, 1, 16)):
        arrived(lg.at[me.right_at(x, k, 1)], lr.at[i])
    queries(0)
    queries(1)
    ring(2, 1)
    send(right, moved, ms.at[0], ms.at[1], l, ahead)
    send(state, moved_state, ms.at[2], ms.at[3], l, ahead)
    queries(2)
    queries(3)
    scores(0)
    from_negatives(0)
    scores(1)
    ring(3, 0)
    scores(-1)
    from_negatives(1, -1)
    turn(2)
    turn(-2)
    gather_targets(2, -2)
    scores(2)
    ring(3, 1)
    scores(-2)
    from_negatives(2, -2)
    turn(3)
    turn(-3)
    gather_targets(3, -3)
    scores(3)
    scores(-3)
    from_negatives(3, -3)
    for k in (0, 1):
        a = me.left_at(4, k)
        arrived(rg.at[a, LOWS], gr.at[14 + 2 * k])
        arrived(rg.at[a, HIGHS], gr.at[15 + 2 * k])
    turn(4)
    gather_targets(4)
    scores(4)

    def positive_grad(t):
        q = qf[:, TILES[t]]
        positive = jnp.sum(q * tt[:, TILES[t]], axis=0, keepdims=True)
        pos_grad = -jax.nn.sigmoid(-positive)
        tg[:, TILES[t]] = (pos_grad * q).astype(BF16)
        return pos_grad

    def query_grad(t):
        g = pos_grads[t] * tt[:, TILES[t]] + gq[:, TILES[t]]
        sg[:, TILES[t]] = back(g, os_[:, TILES[t]]).astype(BF16)
        og[:, TILES[t]] = back(g, ss_[:, TILES[t]]).astype(BF16)

    def right_grad(d):
        zi = mod(me.z + d, 8)
        at = pl.ds(rows_of(d), J)
        part = dot_nt(qs[...], w[at, :]) + dot_nt(tg[...], oht[at, :])
        rp[2 * zi] = part[:, :B]
        rp[2 * zi + 1] = part[:, B:]

    zto, xto, sign = (zp, zm), (xp, xm), (1, -1)

    pos_grads = [positive_grad(t) for t in range(4)]
    right_grad(4)
    for k in (1, 0):
        rfar[k] = rp[me.left_at(4, k)].astype(BF16)
    for k in (1, 0):
        for side in (0, 1):
            rows = pl.ds(0, LOW if side == 0 else HIGH)
            send(rfar.at[k, PART[side]], rb_half.at[side, k, rows], zs.at[side, 3, k], zr.at[side, 3, k], zto[side], r)

    def right_step(d, k):
        for side, at in ((0, me.left_at(d, k)), (1, me.left_at(-d, k))):
            mine = rp[at]
            if d == 3:
                rows = pl.ds(0, LOW if side == 0 else HIGH)
                arrived(rb_half.at[side, k, rows], zr.at[side, 3, k])
                got = rb_half[side, k, rows].astype(F32)
                if side == 0:
                    total = jnp.concatenate([mine[:LOW] + got, mine[LOW:]], axis=0)
                else:
                    total = jnp.concatenate([mine[:LOW], mine[LOW:] + got], axis=0)
            else:
                arrived(rb.at[side, d, k], zr.at[side, d, k])
                total = mine + rb[side, d, k].astype(F32)
            rstage[side, d - 1, k] = total.astype(BF16)
            send(rstage.at[side, d - 1, k], rb.at[side, d - 1, k], zs.at[side, d - 1, k], zr.at[side, d - 1, k], zto[side], r)

    from_negatives(4)
    for t in range(4):
        query_grad(t)
    part = dot_nt(ohr[...], og[...]).astype(BF16)
    for i in range(N):
        pp[i] = part[i * 16 : i * 16 + 16]
    for i in range(1, N):
        to = mod(r + i, N)
        send(pp.at[to], pbuf.at[i], ps.at[i], pr.at[i], l, to)
    right_grad(3)
    right_grad(-3)

    order = ((2, 0), (2, 1), (1, 0), (-1, 0), (1, 1), (-1, 1), (0, 0), (0, 1))

    def left_grad(n):
        x, k = order[n]
        g = lax.div(me.right_at(x, k), 2)
        part = dot_nt(sg[...], ohs[pl.ds(pl.multiple_of(g * J, J), J), :])
        lp[2 * g] = part[:, :B]
        lp[2 * g + 1] = part[:, B:]
        cst[n] = lp[me.right_at(x, k, 1)].astype(BF16)
        send(cst.at[n], cbuf.at[n], cs.at[n], cr.at[n], l, co)

    def chip_sum(n):
        x, k = order[n]
        arrived(cbuf.at[n], cr.at[n])
        return lp[me.right_at(x, k)] + cbuf[n].astype(F32)

    for n in range(4):
        left_grad(n)
    right_step(3, 1)
    right_step(3, 0)
    left_grad(4)
    left_grad(5)
    right_grad(2)
    right_grad(-2)
    total = pp[r].astype(F32)
    for i in range(1, N):
        arrived(pbuf.at[i], pr.at[i])
        total += pbuf[i].astype(F32)
    for i in range(N):
        prow[i] = total[i : i + 1]
    for i in range(1, N):
        to = mod(l + i, N)
        send(prow.at[to], qbuf.at[i], qsm.at[i], qrm.at[i], to, r)

    for k in (1, 0):
        lstage[0, k] = chip_sum(k).astype(BF16)
        for side in (0, 1):
            rows = pl.ds(0, LOW if side == 0 else HIGH)
            send(lstage.at[0, k, PART[side]], lb_half.at[side, k, rows], xs.at[side, 1, k], xr.at[side, 1, k], l, xto[side])
    left_grad(6)
    left_grad(7)
    right_grad(1)
    right_grad(-1)
    right_step(2, 1)
    right_step(2, 0)
    right_grad(0)
    for k in (1, 0):
        for side in (0, 1):
            total = chip_sum(2 + 2 * k + side)
            rows = pl.ds(0, LOW if side == 0 else HIGH)
            arrived(lb_half.at[side, k, rows], xr.at[side, 1, k])
            got = lb_half[side, k, rows].astype(F32)
            if side == 0:
                total = jnp.concatenate([total[:LOW] + got, total[LOW:]], axis=0)
            else:
                total = jnp.concatenate([total[:LOW], total[LOW:] + got], axis=0)
            lstage[1 + side, k] = total.astype(BF16)
            send(lstage.at[1 + side, k], lb.at[side, k], xs.at[side, 0, k], xr.at[side, 0, k], l, xto[side])
    total = prow[l]
    for i in range(1, N):
        arrived(qbuf.at[i], qrm.at[i])
        total += qbuf[i]
    qrow[l] = total
    for i in range(1, N):
        to = mod(l + i, N)
        send(qrow.at[l], qrow.at[l], fs.at[i], fr.at[i], to, r)

    right_step(1, 1)
    right_step(1, 0)

    for i in range(1, N):
        arrived(qrow.at[mod(l - i, N)], fr.at[i])
    total = jnp.concatenate([qrow[i] for i in range(N)], axis=0)
    fown[...] = total.astype(BF16)
    psum[r] = fown[...]
    for i in range(1, N):
        to = mod(r + i, N)
        send(fown, fbuf.at[i], ps.at[N + i], pr.at[N + i], l, to)

    other = rp[me.left_at(0, 1)]
    for side in (0, 1):
        arrived(rb.at[side, 0, 1], zr.at[side, 0, 1])
        other += rb[side, 0, 1].astype(F32)
    ybuf[0] = other.astype(BF16)
    send(ybuf.at[0], ybuf.at[1], ts.at[1], tr.at[1], l_other, r)
    other = chip_sum(7)
    for side in (0, 1):
        arrived(lb.at[side, 1], xr.at[side, 0, 1])
        other += lb[side, 1].astype(F32)
    lx[...] = other.astype(BF16)
    send(lx, lybuf, ts.at[0], tr.at[0], l, yo)
    total = chip_sum(6)
    for side in (0, 1):
        arrived(lb.at[side, 0], xr.at[side, 0, 0])
        total += lb[side, 0].astype(F32)
    lsum[...] = total

    total = rp[l]
    for side in (0, 1):
        arrived(rb.at[side, 0, 0], zr.at[side, 0, 0])
        total += rb[side, 0, 0].astype(F32)
    arrived(ybuf.at[1], tr.at[1])
    rsum[...] = total + ybuf[1].astype(F32)
    arrived(lybuf, tr.at[0])
    lsum[...] += lybuf[...].astype(F32)
    arrived(moved, ms.at[1])
    arrived(moved_state, ms.at[3])
    for i in range(1, N):
        arrived(fbuf.at[i], pr.at[N + i])
        psum[mod(r - i, N)] = fbuf[i]
    for copy in sends:
        copy.wait_send()


def bucket(left, right, state, relation, src, rid, tgt, neg):
    vm = pl.BlockSpec(memory_space=pltpu.VMEM)
    dma = pltpu.SemaphoreType.DMA
    blocks = pltpu.VMEM((N, W, B), BF16)
    return pl.pallas_call(
        bucket_kernel,
        out_shape=(
            jax.ShapeDtypeStruct((W, B), F32),
            jax.ShapeDtypeStruct((W, B), F32),
            jax.ShapeDtypeStruct((N, 16, W), BF16),
            jax.ShapeDtypeStruct((W, B), F32),
            jax.ShapeDtypeStruct((1, B), F32),
        ),
        in_specs=[vm] * 8,
        out_specs=(vm,) * 5,
        scratch_shapes=[
            pltpu.VMEM((W, B), BF16),
            pltpu.VMEM((W, B), BF16),
            blocks,
            blocks,
            pltpu.VMEM((N * B, W), BF16),
            pltpu.VMEM((W, 256), BF16),
            pltpu.VMEM((N * B, E), BF16),
            pltpu.VMEM((256, E), BF16),
            pltpu.VMEM((N * B, E), BF16),
            pltpu.VMEM((W, E), BF16),
            pltpu.VMEM((W, E), F32),
            pltpu.VMEM((W, E), F32),
            pltpu.VMEM((W, E), BF16),
            pltpu.VMEM((W, E), BF16),
            pltpu.VMEM((2, N * B, B), F32),
            pltpu.VMEM((N, W, B), F32),
            pltpu.VMEM((N, W, B), F32),
            pltpu.VMEM((N, 16, W), BF16),
            pltpu.VMEM((N * B, E), BF16),
            pltpu.VMEM((W, E), F32),
            pltpu.VMEM((W, E), F32),
            pltpu.VMEM((W, E), F32),
            pltpu.VMEM((W, E), BF16),
            pltpu.VMEM((2, 2, LOW, B), BF16),
            pltpu.VMEM((2, 3, 2, W, B), BF16),
            pltpu.VMEM((2, 3, 2, W, B), BF16),
            pltpu.VMEM((2, W, B), BF16),
            pltpu.VMEM((2, W, B), BF16),
            pltpu.VMEM((8, W, B), BF16),
            pltpu.VMEM((8, W, B), BF16),
            pltpu.VMEM((2, 2, LOW, B), BF16),
            pltpu.VMEM((2, 2, W, B), BF16),
            pltpu.VMEM((3, 2, W, B), BF16),
            pltpu.VMEM((W, B), BF16),
            pltpu.VMEM((W, B), BF16),
            pltpu.VMEM((N, 16, W), BF16),
            pltpu.VMEM((N, 1, W), F32),
            pltpu.VMEM((N, 1, W), F32),
            pltpu.VMEM((N, 1, W), F32),
            pltpu.VMEM((N, 16, W), BF16),
            pltpu.VMEM((16, W), BF16),
            dma((18,)), dma((18,)), dma((17,)), dma((17,)), dma((4,)),
            dma((2, 4, 2)), dma((2, 4, 2)),
            dma((8,)), dma((8,)),
            dma((2, 2, 2)), dma((2, 2, 2)),
            dma((2 * N,)), dma((2 * N,)),
            dma((N,)), dma((N,)),
            dma((N,)), dma((N,)),
            dma((3,)), dma((2,)),
        ],
        compiler_params=pltpu.CompilerParams(collective_id=0, has_side_effects=True, vmem_limit_bytes=VMEM_LIMIT),
        name="bucket_round",
    )(left, right, state, relation, src, rid, tgt, neg)


def update_kernel(left, left_state, lsum, moved, moved_state, rsum, rel, rel_state, psum, lo, lso, ro, rso, po, pso):
    for table, state, grad, out, state_out in (
        (left, left_state, lsum[...], lo, lso),
        (moved, moved_state, rsum[...], ro, rso),
        (rel, rel_state, psum[...].reshape(256, W).astype(F32).T, po, pso),
    ):
        new = state[...] + jnp.sum(grad * grad, axis=0, keepdims=True) * (1.0 / W)
        state_out[...] = new
        out[...] = table[...] - LEARN_RATE * grad / jnp.sqrt(new)


def update(*args):
    vm = pl.BlockSpec(memory_space=pltpu.VMEM)
    return pl.pallas_call(
        update_kernel,
        out_shape=(
            jax.ShapeDtypeStruct((W, B), F32),
            jax.ShapeDtypeStruct((1, B), F32),
            jax.ShapeDtypeStruct((W, B), F32),
            jax.ShapeDtypeStruct((1, B), F32),
            jax.ShapeDtypeStruct((W, 256), F32),
            jax.ShapeDtypeStruct((1, 256), F32),
        ),
        in_specs=[vm] * 9,
        out_specs=(vm,) * 6,
        name="update_tables",
    )(*args)


def per_device(
    left_table,
    left_state,
    right_table,
    right_state,
    relation_table,
    relation_state,
    source_ids,
    target_ids,
    relation_ids,
    negative_ids,
):
    row = lambda state: state.reshape(1, -1)
    lsum, rsum, psum, moved, moved_state = bucket(
        left_table.T, right_table.T, row(right_state), relation_table.T, source_ids, relation_ids, target_ids, negative_ids
    )
    left_new, left_state_new, right_new, right_state_new, relation_new, relation_state_new = update(
        left_table.T, row(left_state), lsum, moved, moved_state, rsum, relation_table.T, row(relation_state), psum
    )
    flat = lambda state: state.reshape(-1)
    return (left_new.T, flat(left_state_new), right_new.T, flat(right_state_new), relation_new.T, flat(relation_state_new))


def solution(mesh):
    return jax.shard_map(
        per_device,
        mesh=mesh,
        in_specs=(
            P(("left", "right"), None),
            P(("left", "right")),
            P(("left", "right"), None),
            P(("left", "right")),
            P(),
            P(),
            P("left", "right", None),
            P("left", "right", None),
            P("left", "right", None),
            P("left", "right", None, None),
        ),
        out_specs=(
            P(("left", "right"), None),
            P(("left", "right")),
            P(("left", "right"), None),
            P(("left", "right")),
            P(),
            P(),
        ),
        check_vma=False,
    )
```
